512 devices in a mesh: ty: 32 (over x, z), tx: 16 (over y, core).
Axes of the slice: x: 4, y: 8, z: 8, core: 2. Of those that a mesh axis runs over, the one named last changes fastest.
Arguments:
- stored_eastward_flow: float32 [30, 256, 2048], P(None, 'ty', 'tx'), may hold values from -6 to 6
- stored_northward_flow: float32 [30, 256, 2048], P(None, 'ty', 'tx'), may hold values from -6 to 6
- stored_heat_content: float32 [30, 256, 2048], P(None, 'ty', 'tx'), may hold values from -6 to 6
- ocean_layer_tally: int32 [256, 2048], P('ty', 'tx'), may hold values from 0 to 30, as said below
- eastward_flow_sensitivity: float32 [30, 256, 2048], P(None, 'ty', 'tx'), may hold values from -6 to 6
- northward_flow_sensitivity: float32 [30, 256, 2048], P(None, 'ty', 'tx'), may hold values from -6 to 6
- scalar_content_sensitivity: float32 [30, 256, 2048], P(None, 'ty', 'tx'), may hold values from -6 to 6
- elevation_sensitivity: float32 [256, 2048], P('ty', 'tx'), may hold values from -6 to 6
Outputs:
- u_gradient: float32 [30, 256, 2048], P(None, 'ty', 'tx')
- v_gradient: float32 [30, 256, 2048], P(None, 'ty', 'tx')
- t_gradient: float32 [30, 256, 2048], P(None, 'ty', 'tx')
- eta_gradient: float32 [256, 2048], P('ty', 'tx')
The draws below stay inside these ranges and needn't reach their ends.
Inputs may be any that keep to these rules, and one draw needn't show every extreme that they name: `ocean_layer_tally`: the number of wet levels of each column; 0 marks land.
All inputs are finite; a program needn't handle non-finite values.
Results may differ from the reference program's by a relative error of at most 0.0001.
Values sent between devices are 32-bit elements; how exact they have to be, the bound alone decides.
A program may use at most 64 MiB of HBM per device.

```python
import jax
import jax.numpy as jnp
from jax import lax

DEPTH_LAYERS = 30
ITERS = 4
MESH_NORTHWARD_N = 256
MESH_EASTWARD_N = 2048


def draw_ocean_layer_tally(key, part):
    key_depth, key_land = jax.random.split(key)
    row_number = jnp.arange(MESH_NORTHWARD_N)[:, None]
    depth_limit = 1 + (DEPTH_LAYERS - 1) * (row_number + 1) // MESH_NORTHWARD_N
    base_depth = jax.random.randint(key_depth, (MESH_NORTHWARD_N, MESH_EASTWARD_N), 1, DEPTH_LAYERS + 1)
    column_depth = jnp.minimum(base_depth, depth_limit)
    blocks = jax.random.randint(key_land, ((MESH_NORTHWARD_N + 15) // 16, (MESH_EASTWARD_N + 63) // 64), 0, 4)
    land_cell = jnp.repeat(jnp.repeat(blocks, 16, axis=0), 64, axis=1)[:MESH_NORTHWARD_N, :MESH_EASTWARD_N] == 0
    column_depth = jnp.where(land_cell, 0, column_depth)
    column_depth = column_depth.at[MESH_NORTHWARD_N - 1, MESH_EASTWARD_N - 1].set(DEPTH_LAYERS)
    column_depth = column_depth.at[0, 0].set(0)
    return column_depth.astype(jnp.int32)


def block_scale(stream_key, dims, cuts, least, top_value):
    factor_of, own = 1.0, jax.random.fold_in(stream_key, 6)
    for dim, blocks in cuts:
        steps = jnp.exp(jax.random.uniform(jax.random.fold_in(own, dim), (blocks,), jnp.float32, least / len(cuts), top_value / len(cuts)))
        factor_of = factor_of * jnp.repeat(steps, dims[dim] // blocks).reshape([-1 if axis == dim else 1 for axis in range(len(dims))])
    return factor_of


def centred(own_key, dims, width, limit, pieces=(), kind=jnp.bfloat16):
    values = jax.random.normal(own_key, dims, jnp.float32) * width
    if len(pieces) > 0:
        values = block_scale(own_key, dims, pieces, -0.22, 0.18) * values
    return jnp.clip(values, min=-limit, max=limit).astype(kind)


def setup_inputs(seed: int = 0) -> dict:
    splits = jax.random.split(jax.random.key(seed), 9)
    stored_eastward_flow = centred(splits[0], (DEPTH_LAYERS, MESH_NORTHWARD_N, MESH_EASTWARD_N), 1.0, 6.0, ((1, 32), (2, 16)), jnp.float32)
    stored_northward_flow = centred(splits[1], (DEPTH_LAYERS, MESH_NORTHWARD_N, MESH_EASTWARD_N), 1.0, 6.0, ((1, 32), (2, 16)), jnp.float32)
    stored_heat_content = centred(splits[2], (DEPTH_LAYERS, MESH_NORTHWARD_N, MESH_EASTWARD_N), 1.0, 6.0, ((1, 32), (2, 16)), jnp.float32)
    ocean_layer_tally = draw_ocean_layer_tally(jax.random.fold_in(splits[8], 71), 0)
    eastward_flow_sensitivity = centred(splits[4], (DEPTH_LAYERS, MESH_NORTHWARD_N, MESH_EASTWARD_N), 1.0, 6.0, ((1, 32), (2, 16)), jnp.float32)
    northward_flow_sensitivity = centred(splits[5], (DEPTH_LAYERS, MESH_NORTHWARD_N, MESH_EASTWARD_N), 1.0, 6.0, ((1, 32), (2, 16)), jnp.float32)
    scalar_content_sensitivity = centred(splits[6], (DEPTH_LAYERS, MESH_NORTHWARD_N, MESH_EASTWARD_N), 1.0, 6.0, ((1, 32), (2, 16)), jnp.float32)
    elevation_sensitivity = centred(splits[7], (MESH_NORTHWARD_N, MESH_EASTWARD_N), 1.0, 6.0, ((0, 32), (1, 16)), jnp.float32)
    return {"stored_eastward_flow": stored_eastward_flow, "stored_northward_flow": stored_northward_flow, "stored_heat_content": stored_heat_content, "ocean_layer_tally": ocean_layer_tally, "eastward_flow_sensitivity": eastward_flow_sensitivity, "northward_flow_sensitivity": northward_flow_sensitivity, "scalar_content_sensitivity": scalar_content_sensitivity, "elevation_sensitivity": elevation_sensitivity}


ADVECT = 0.1
GRAVITY_DT = 0.1
STEP_DT = 1.0

def wet_cells(count_float, levels):
    level_index = jnp.arange(levels).astype(jnp.float32)
    return (level_index[:, None, None] < count_float[None]).astype(jnp.float32)

def tendencies(u_input, v_input, t_input, wet_cell, coriolis_u, coriolis_v):
    row_count = u_input.shape[1] - 4
    col_count = u_input.shape[2] - 4

    def offset_view(source, shift_row, shift_col):
        return source[:, 2 + shift_row:2 + shift_row + row_count, 2 + shift_col:2 + shift_col + col_count]

    def mask_u(shift_row, shift_col):
        return offset_view(wet_cell, shift_row, shift_col) * offset_view(wet_cell, shift_row, shift_col - 1)

    def mask_v(shift_row, shift_col):
        return offset_view(wet_cell, shift_row, shift_col) * offset_view(wet_cell, shift_row - 1, shift_col)

    def flux_x(shift_col):
        face_value = (7.0 * (offset_view(t_input, 0, shift_col) + offset_view(t_input, 0, shift_col - 1)) - (offset_view(t_input, 0, shift_col + 1) + offset_view(t_input, 0, shift_col - 2))) / 12.0
        return mask_u(0, shift_col) * offset_view(u_input, 0, shift_col) * face_value

    def flux_y(shift_row):
        face_value = (7.0 * (offset_view(t_input, shift_row, 0) + offset_view(t_input, shift_row - 1, 0)) - (offset_view(t_input, shift_row + 1, 0) + offset_view(t_input, shift_row - 2, 0))) / 12.0
        return mask_v(shift_row, 0) * offset_view(v_input, shift_row, 0) * face_value
    t_new = offset_view(t_input, 0, 0) - ADVECT * offset_view(wet_cell, 0, 0) * (flux_x(1) - flux_x(0) + flux_y(1) - flux_y(0))
    u_here = offset_view(u_input, 0, 0)
    v_here = offset_view(v_input, 0, 0)
    v_bar = 0.25 * (v_here + offset_view(v_input, 1, 0) + offset_view(v_input, 0, -1) + offset_view(v_input, 1, -1))
    u_bar = 0.25 * (u_here + offset_view(u_input, 0, 1) + offset_view(u_input, -1, 0) + offset_view(u_input, -1, 1))
    u_star = u_here + ADVECT * mask_u(0, 0) * (coriolis_u * v_bar - u_here * 0.5 * (offset_view(u_input, 0, 1) - offset_view(u_input, 0, -1)) - v_bar * 0.5 * (offset_view(u_input, 1, 0) - offset_view(u_input, -1, 0)))
    v_star = v_here + ADVECT * mask_v(0, 0) * (-coriolis_v * u_bar - u_bar * 0.5 * (offset_view(v_input, 0, 1) - offset_view(v_input, 0, -1)) - v_here * 0.5 * (offset_view(v_input, 1, 0) - offset_view(v_input, -1, 0)))
    return (u_star, v_star, t_new)

def surface_apply(rimmed, depth_u, depth_v):
    centre = rimmed[1:-1, 1:-1]
    east = rimmed[1:-1, 2:]
    west = rimmed[1:-1, :-2]
    north = rimmed[2:, 1:-1]
    south = rimmed[:-2, 1:-1]
    return centre - GRAVITY_DT * STEP_DT * (depth_u[1:-1, 2:] * (east - centre) - depth_u[1:-1, 1:-1] * (centre - west) + depth_v[2:, 1:-1] * (north - centre) - depth_v[1:-1, 1:-1] * (centre - south))

def reference(stored_eastward_flow, stored_northward_flow, stored_heat_content, ocean_layer_tally, eastward_flow_sensitivity, northward_flow_sensitivity, scalar_content_sensitivity, elevation_sensitivity):
    levels, row_count, col_count = stored_eastward_flow.shape
    count_float = ocean_layer_tally.astype(jnp.float32)
    wet_padded = wet_cells(jnp.pad(count_float, 2), levels)
    row_index = jnp.arange(row_count).astype(jnp.float32)[:, None]
    coriolis_u = 0.5 + (row_index + 0.5) / row_count
    coriolis_v = 0.5 + row_index / row_count
    thickness = (1.0 + jnp.arange(levels).astype(jnp.float32) / levels)[:, None, None]
    inner_wet = wet_padded[:, 1:-1, 1:-1]
    u_mask = inner_wet * wet_padded[:, 1:-1, :-2]
    v_mask = inner_wet * wet_padded[:, :-2, 1:-1]
    depth_u = lax.optimization_barrier(jnp.sum(thickness * u_mask, axis=0))
    depth_v = lax.optimization_barrier(jnp.sum(thickness * v_mask, axis=0))
    pad_one = ((0, 0), (1, 1), (1, 1))
    col_u = lax.optimization_barrier(jnp.sum(u_mask * jnp.pad(eastward_flow_sensitivity, pad_one), axis=0))
    col_v = lax.optimization_barrier(jnp.sum(v_mask * jnp.pad(northward_flow_sensitivity, pad_one), axis=0))
    surface_load = elevation_sensitivity + GRAVITY_DT * (col_u[1:-1, 2:] - col_u[1:-1, 1:-1] + col_v[2:, 1:-1] - col_v[1:-1, 1:-1])

    def operate(direction):
        return surface_apply(jnp.pad(direction, 1), depth_u, depth_v)
    solution = jnp.zeros_like(surface_load)
    residual = surface_load
    direction = surface_load
    norm_now = jnp.sum(residual * residual)
    for iteration in range(ITERS):
        applied = operate(direction)
        step_length = norm_now / jnp.sum(direction * applied)
        solution = solution + step_length * direction
        residual = residual - step_length * applied
        norm_next = jnp.sum(residual * residual)
        direction = residual + norm_next / norm_now * direction
        norm_now = norm_next
    solution_pad = jnp.pad(solution, 1)
    u_cotangent = eastward_flow_sensitivity + STEP_DT * thickness * u_mask[:, 1:-1, 1:-1] * (solution - solution_pad[1:-1, :-2])[None]
    v_cotangent = northward_flow_sensitivity + STEP_DT * thickness * v_mask[:, 1:-1, 1:-1] * (solution - solution_pad[:-2, 1:-1])[None]
    pad_two = ((0, 0), (2, 2), (2, 2))

    def advance_ocean_once(u_input, v_input, t_input):
        return tendencies(jnp.pad(u_input, pad_two), jnp.pad(v_input, pad_two), jnp.pad(t_input, pad_two), wet_padded, coriolis_u, coriolis_v)
    advance_results, backward_chain_rule = jax.vjp(advance_ocean_once, stored_eastward_flow, stored_northward_flow, stored_heat_content)
    gradients = backward_chain_rule((u_cotangent, v_cotangent, scalar_content_sensitivity))
    return (gradients[0], gradients[1], gradients[2], solution)
```

```python
import functools

import jax
import jax.numpy as jnp
from jax import lax
from jax.experimental import pallas as pl
from jax.experimental.pallas import tpu as pltpu
from jax.sharding import PartitionSpec as P

MESH = pl.DeviceIdType.MESH
ADVECT = 0.1
GRAVITY_DT = 0.1
ROWS, COLS = 8, 128

E, W, N, S, NE, NW, SE, SW = range(8)
WAY = ((0, 1), (0, -1), (1, 0), (-1, 0), (1, 1), (1, -1), (-1, 1), (-1, -1))
OPPOSITE = (W, E, S, N, SW, SE, NW, NE)
COLUMN_SLOT = {E: 0, W: 1, NE: 2, NW: 3, SE: 4, SW: 5}


def turn(x, shift, axis):
    return pltpu.roll(x, shift % x.shape[axis], axis)


def east(x):
    return turn(x, -1, 1)


def west(x):
    return turn(x, 1, 1)


def north(x):
    return turn(x, -1, 0)


def south(x):
    return turn(x, 1, 0)


def tile(a, b, c, d):
    return jnp.concatenate(
        [jnp.concatenate([a, b], axis=1), jnp.concatenate([c, d], axis=1)], axis=0
    )


def kernel(
    levels, n_ty, n_tx,
    u_ref, v_ref, t_ref, count_ref, us_ref, vs_ref, ts_ref, elev_ref,
    gu_ref, gv_ref, gt_ref, eta_ref,
    count_in, elev_in, col_out, col_in,
    colp_out, colp_in, rown_out, rows_out, rown2_out, rows2_out,
    rown_in, rows_in, rown2_in, rows2_in,
    sides, corners, mine, tx_in, ty_in,
    k_pu, k_pv, k_b, k_qv, k_qu, k_c, k_u, k_v,
    hop_send, hop_recv, tx_send, tx_recv, ty_send, ty_recv,
):
    r, c = lax.axis_index("ty"), lax.axis_index("tx")
    total_rows = ROWS * n_ty

    def at(d):
        dy, dx = WAY[d]
        return (lax.rem(r + dy + n_ty, n_ty), lax.rem(c + dx + n_tx, n_tx))

    def hop(number, src, dst, d):
        return pltpu.make_async_remote_copy(
            src_ref=src, dst_ref=dst,
            send_sem=hop_send.at[number], recv_sem=hop_recv.at[number],
            device_id=at(d), device_id_type=MESH,
        )

    barrier = pltpu.get_barrier_semaphore()

    def greet_tx(o, carry):
        pl.semaphore_signal(barrier, inc=1, device_id=(r, lax.rem(c + o, n_tx)), device_id_type=MESH)
        return carry

    def greet_ty(o, carry):
        pl.semaphore_signal(barrier, inc=1, device_id=(lax.rem(r + o, n_ty), c), device_id_type=MESH)
        return carry

    lax.fori_loop(1, n_ty, greet_ty, 0)
    lax.fori_loop(1, n_tx, greet_tx, 0)
    for d in (NE, NW, SE, SW):
        pl.semaphore_signal(barrier, inc=1, device_id=at(d), device_id_type=MESH)

    lane = lax.broadcasted_iota(jnp.int32, (ROWS, COLS), 1)
    sub = lax.broadcasted_iota(jnp.int32, (ROWS, COLS), 0)
    fields = (u_ref, v_ref, us_ref, vs_ref, t_ref, ts_ref)

    def pack(k, packed):
        x = [f[k] for f in fields]
        here = lax.div(lane, 4) == k
        shift = lax.rem(4 * k + 2, COLS)
        packed = tuple(jnp.where(here, pltpu.roll(a, shift, 1), b) for a, b in zip(x, packed))
        u, v, us, vs, t, ts = x
        rown_out[k] = jnp.where(
            sub >= 6, u, jnp.where(sub >= 4, turn(v, -2, 0), jnp.where(sub >= 2, turn(t, 4, 0), turn(ts, 2, 0)))
        )
        rows_out[k] = jnp.where(
            sub < 2, u, jnp.where(sub < 4, turn(v, 2, 0), jnp.where(sub < 6, turn(t, 4, 0), turn(ts, -2, 0)))
        )
        rown2_out[k] = jnp.concatenate([us[7:8], vs[7:8]], axis=0)
        rows2_out[k] = jnp.concatenate([us[0:1], vs[0:1]], axis=0)
        return packed

    packed = lax.fori_loop(0, levels, pack, tuple(jnp.zeros((ROWS, COLS), jnp.float32) for _ in fields))
    for f in range(6):
        colp_out[f] = packed[f]

    pl.semaphore_wait(barrier, (n_tx - 1) + (n_ty - 1) + 4)

    first = [hop(d, count_ref, count_in.at[OPPOSITE[d]], d) for d in range(8)]
    first += [hop(8 + d, elev_ref, elev_in.at[OPPOSITE[d]], d) for d in range(8)]
    for copy in first:
        copy.start()

    wide_row = lax.broadcasted_iota(jnp.int32, (3 * ROWS, 2 * COLS), 0)
    wide_col = lax.broadcasted_iota(jnp.int32, (3 * ROWS, 2 * COLS), 1)
    row_at = r * ROWS + jnp.where(wide_row < 16, wide_row, wide_row - 24)
    col_at = c * COLS + jnp.where(wide_col < 192, wide_col, wide_col - 256)
    inside = (row_at >= 0) & (row_at < total_rows) & (col_at >= 0) & (col_at < COLS * n_tx)

    def around(own, part):
        rim = [jnp.where(lane < 64, part(a), part(b)) for a, b in ((E, W), (NE, NW), (SE, SW))]
        return jnp.concatenate(
            [jnp.concatenate([a, b], axis=1) for a, b in zip((own, part(N), part(S)), rim)], axis=0
        )

    for copy in first:
        copy.wait_recv()
    count = jnp.where(inside, around(count_ref[...], lambda d: count_in[d]).astype(jnp.float32), 0.0)
    count_u = jnp.minimum(count, west(count))
    count_v = jnp.minimum(count, south(count))
    depth_u = count_u + count_u * (count_u - 1.0) * (0.5 / levels)
    depth_v = count_v + count_v * (count_v - 1.0) * (0.5 / levels)

    own_u, own_v = count_u[:ROWS, :COLS], count_v[:ROWS, :COLS]
    col_u = jnp.zeros((ROWS, COLS), jnp.float32)
    col_v = jnp.zeros((ROWS, COLS), jnp.float32)
    for k in range(levels):
        col_u = col_u + jnp.where(own_u > float(k), us_ref[k], 0.0)
        col_v = col_v + jnp.where(own_v > float(k), vs_ref[k], 0.0)
    col_out[0] = col_u
    col_out[1] = col_v
    second = [hop(16 + d, col_out, col_in.at[OPPOSITE[d]], d) for d in range(8)]
    for copy in second:
        copy.start()

    third = [
        hop(24, rown_out, rows_in, N), hop(25, rows_out, rown_in, S),
        hop(26, rown2_out, rows2_in, N), hop(27, rows2_out, rown2_in, S),
    ]
    for i, d in enumerate((E, W, NE, NW, SE, SW)):
        slot = colp_in.at[COLUMN_SLOT[OPPOSITE[d]]]
        whole = d in (E, W)
        third.append(
            hop(28 + i, colp_out if whole else colp_out.at[0:4], slot if whole else slot.at[0:4], d)
        )
    for copy in third:
        copy.start()

    def squeeze(x):
        low = lax.broadcasted_iota(jnp.int32, (ROWS, 2 * COLS), 0) < 4
        return jnp.concatenate([x[:ROWS], jnp.where(low, x[ROWS : 2 * ROWS], x[2 * ROWS :])], axis=0)

    cu, cv = squeeze(count_u), squeeze(count_v)
    row16 = lax.broadcasted_iota(jnp.int32, (2 * ROWS, 2 * COLS), 0)
    row16 = (r * ROWS + jnp.where(row16 < 12, row16, row16 - 16)).astype(jnp.float32)
    fu = 0.5 + (row16 + 0.5) / total_rows
    fv = 0.5 + row16 / total_rows

    for copy in second:
        copy.wait_recv()
    col_u = jnp.where(inside, around(col_out[0], lambda d: col_in[d, 0]), 0.0)
    col_v = jnp.where(inside, around(col_out[1], lambda d: col_in[d, 1]), 0.0)
    elevation = around(elev_ref[...], lambda d: elev_in[d])
    load = jnp.where(
        inside, elevation + GRAVITY_DT * (east(col_u) - col_u + north(col_v) - col_v), 0.0
    )

    def operate(p):
        flow_u = depth_u * (p - west(p))
        flow_v = depth_v * (p - south(p))
        return p - GRAVITY_DT * (east(flow_u) - flow_u + north(flow_v) - flow_v)

    sub16 = lax.broadcasted_iota(jnp.int32, (16, COLS), 0)
    lane16 = lax.broadcasted_iota(jnp.int32, (16, COLS), 1)
    lane1 = lax.broadcasted_iota(jnp.int32, (1, COLS), 1)

    def dots(pairs):
        sums = jnp.zeros((16, COLS), jnp.float32)
        for m, (a, b) in enumerate(pairs):
            part = jnp.sum(a[:ROWS, :COLS] * b[:ROWS, :COLS], axis=0, keepdims=True)
            sums = jnp.where(sub16 == m, part, sums)
        sums = jnp.sum(sums, axis=1, keepdims=True)
        return jnp.sum(jnp.where(lane16 == sub16, sums, 0.0), axis=0, keepdims=True)

    def tx_copy(i, target, slot, sem):
        return pltpu.make_async_remote_copy(
            src_ref=mine.at[2 * i], dst_ref=tx_in.at[i, slot],
            send_sem=tx_send.at[i, sem], recv_sem=tx_recv.at[i, slot],
            device_id=(r, target), device_id_type=MESH,
        )

    def ty_copy(i, target, slot, sem):
        return pltpu.make_async_remote_copy(
            src_ref=mine.at[2 * i + 1], dst_ref=ty_in.at[i, slot],
            send_sem=ty_send.at[i, sem], recv_sem=ty_recv.at[i, slot],
            device_id=(target, c), device_id_type=MESH,
        )

    def spread(i, copy, me, n):
        def body(o, carry):
            copy(i, lax.rem(me + o, n), me, o).start()
            return carry

        lax.fori_loop(1, n, body, 0)

    def gather(i, copy, me, n):
        def body(o, carry):
            other = lax.rem(me + o, n)
            copy(i, other, other, o).wait_recv()
            return carry

        lax.fori_loop(1, n, body, 0)

    def drain(i, copy, me, n):
        def body(o, carry):
            copy(i, lax.rem(me + o, n), me, o).wait_send()
            return carry

        lax.fori_loop(1, n, body, 0)

    def total(i, row, cover_tx, cover_ty):
        mine[2 * i] = row
        spread(i, tx_copy, c, n_tx)
        tx_in[i, c] = row
        cover_tx()
        gather(i, tx_copy, c, n_tx)
        row = jnp.sum(tx_in[i], axis=0)
        mine[2 * i + 1] = row
        spread(i, ty_copy, r, n_ty)
        ty_in[i, r] = row
        cover_ty()
        gather(i, ty_copy, r, n_ty)
        return jnp.sum(ty_in[i], axis=0)

    def pick(row, m):
        return jnp.sum(jnp.where(lane1 == m, row, 0.0), axis=1, keepdims=True)

    def spread_out(px, pb, pv, qv, qc, qu):
        c1 = qc + north(qc)
        b1 = pb + south(pb)
        gu = 0.5 * (east(px) - west(px) + north(pv) - south(pv)) + 0.25 * (c1 + west(c1))
        gv = 0.5 * (north(qv) - south(qv) + east(qu) - west(qu)) + 0.25 * (b1 + east(b1))
        return gu[:ROWS, :COLS], gv[:ROWS, :COLS]

    inner = lax.rem(lane, 4) < 2
    low8 = sub < 4
    beside = jnp.where(inner, c, n_tx - 1 - c) > 0
    beyond = jnp.where(low8, n_ty - 1 - r, r) > 0

    def receive():
        for copy in third:
            copy.wait_recv()
        for f in range(6):
            side = jnp.where(inner, colp_in[COLUMN_SLOT[W], f], colp_in[COLUMN_SLOT[E], f])
            sides[f] = jnp.where(beside, side, 0.0)
        for f in range(4):
            upper = jnp.where(inner, colp_in[COLUMN_SLOT[NW], f], colp_in[COLUMN_SLOT[NE], f])
            lower = jnp.where(inner, colp_in[COLUMN_SLOT[SW], f], colp_in[COLUMN_SLOT[SE], f])
            corners[f] = jnp.where(beside & beyond, jnp.where(low8, upper, lower), 0.0)

    def prepare(k, carry):
        shift = lax.rem(126 - 4 * k + COLS, COLS)
        nb, sb = rown_in[k], rows_in[k]
        nb2, sb2 = rown2_in[k], rows2_in[k]

        def wide(f, ref, ends):
            side = pltpu.roll(sides[f], shift, 1)
            corner = pltpu.roll(corners[f], shift, 1) if f < 4 else side
            return tile(ref[k], side, jnp.where(beyond, ends, 0.0), corner)

        def both(f, ref):
            i = f - 2
            ends = jnp.where(
                low8,
                jnp.broadcast_to(nb2[i : i + 1], (ROWS, COLS)),
                jnp.broadcast_to(sb2[i : i + 1], (ROWS, COLS)),
            )
            return wide(f, ref, ends)

        u = wide(0, u_ref, jnp.where(low8, nb, sb))
        v = wide(1, v_ref, jnp.where(low8, turn(nb, -2, 0), turn(sb, 2, 0)))
        t = wide(4, t_ref, jnp.where(low8, turn(nb, 4, 0), turn(sb, 4, 0)))
        ts = wide(5, ts_ref, jnp.where(low8, turn(nb, 2, 0), turn(sb, -2, 0)))
        us = both(2, us_ref)
        vs = both(3, vs_ref)
        level = k.astype(jnp.float32)
        mask_u = jnp.where(cu > level, ADVECT, 0.0)
        mask_v = jnp.where(cv > level, ADVECT, 0.0)

        flux_x = mask_u * (ts - west(ts))
        flux_y = mask_v * (ts - south(ts))
        x, y = u * flux_x, v * flux_y
        xe, yn = east(x), north(y)
        gt = ts + (
            7.0 * (x + xe + y + yn) - (west(x) + east(xe) + south(y) + north(yn))
        ) * (1.0 / 12.0)
        gt_ref[k] = gt[:ROWS, :COLS]
        tw, tso = west(t), south(t)
        face_x = (7.0 * (t + tw) - (east(t) + west(tw))) * (1.0 / 12.0)
        face_y = (7.0 * (t + tso) - (north(t) + south(tso))) * (1.0 / 12.0)

        ue, vn = east(u), north(v)
        pair_v, pair_u = v + vn, u + ue
        v_bar = 0.25 * (pair_v + west(pair_v))
        u_bar = 0.25 * (pair_u + south(pair_u))
        kpu = mask_u * u
        kpv = mask_u * v_bar
        kb = mask_u * (fu - 0.5 * (north(u) - south(u)))
        kqv = mask_v * v
        kqu = mask_v * u_bar
        kc = -mask_v * (fv + 0.5 * (east(v) - west(v)))
        k_pu[k], k_pv[k], k_b[k] = kpu, kpv, kb
        k_qv[k], k_qu[k], k_c[k] = kqv, kqu, kc
        own_mu, own_mv = mask_u[:ROWS, :COLS], mask_v[:ROWS, :COLS]
        ku = -0.5 * own_mu * (ue - west(u))[:ROWS, :COLS]
        kv = -0.5 * own_mv * (vn - south(v))[:ROWS, :COLS]
        k_u[k] = ku + jnp.where(own_mu > 0.0, 1.0, 0.0)
        k_v[k] = kv + jnp.where(own_mv > 0.0, 1.0, 0.0)
        gu, gv = spread_out(kpu * us, kb * us, kpv * us, kqv * vs, kc * vs, kqu * vs)
        own_us, own_vs = us_ref[k], vs_ref[k]
        gu_ref[k] = gu + own_us + own_us * ku + (flux_x * face_x)[:ROWS, :COLS]
        gv_ref[k] = gv + own_vs + own_vs * kv + (flux_y * face_y)[:ROWS, :COLS]
        return carry

    third_of = levels // 3

    def cover_first():
        receive()
        lax.fori_loop(0, third_of, prepare, 0)

    p0 = load
    p1 = operate(p0)
    p2 = operate(p1)
    row = total(
        0, dots([(p0, p0), (p0, p1), (p1, p1), (p1, p2)]), lambda: None, cover_first
    )
    g00, g01, g11, g12 = [pick(row, m) for m in range(4)]
    alpha1 = g00 / g01
    norm1 = g00 - 2.0 * alpha1 * g01 + alpha1 * alpha1 * g11
    beta1 = norm1 / g00
    e0, e1 = 1.0 + beta1, -alpha1
    alpha2 = norm1 / (e0 * e0 * g01 + 2.0 * e0 * e1 * g11 + e1 * e1 * g12)
    d1 = e0 * p0 + e1 * p1
    x2 = alpha1 * p0 + alpha2 * d1
    w0 = (p0 - alpha1 * p1) - alpha2 * (e0 * p1 + e1 * p2)

    w1 = d1
    w2, w3 = operate(w0), operate(w1)
    w4, w5 = operate(w2), operate(w3)
    row = total(
        1,
        dots(
            [(w0, w0), (w0, w2), (w0, w3), (w1, w3), (w2, w2), (w2, w3), (w3, w3), (w2, w4), (w2, w5), (w3, w5)]
        ),
        lambda: lax.fori_loop(third_of, 2 * third_of, prepare, 0),
        lambda: lax.fori_loop(2 * third_of, levels, prepare, 0),
    )
    h00, h02, h03, h13, h22, h23, h33, h24, h25, h35 = [pick(row, m) for m in range(10)]
    beta2 = h00 / norm1
    twice, square = 2.0 * beta2, beta2 * beta2
    d_a_d = h02 + twice * h03 + square * h13
    ad_ad = h22 + twice * h23 + square * h33
    d_aaa_d = h24 + twice * h25 + square * h35
    r_a_d = h02 + beta2 * h03
    ar_ad = h22 + beta2 * h23
    alpha3 = h00 / d_a_d
    norm3 = h00 - 2.0 * alpha3 * r_a_d + alpha3 * alpha3 * ad_ad
    beta3 = norm3 / h00
    alpha4 = norm3 / (
        h02 + 2.0 * beta3 * r_a_d - 2.0 * alpha3 * ar_ad
        + beta3 * beta3 * d_a_d - 2.0 * alpha3 * beta3 * ad_ad + alpha3 * alpha3 * d_aaa_d
    )
    d2 = w0 + beta2 * w1
    d3 = w0 + beta3 * d2 - alpha3 * (w2 + beta2 * w3)
    answer = x2 + alpha3 * d2 + alpha4 * d3
    eta_ref[...] = answer[:ROWS, :COLS]
    slope_x = squeeze(answer - west(answer))
    slope_y = squeeze(answer - south(answer))

    def finish(k, carry):
        thick = 1.0 + k.astype(jnp.float32) * (1.0 / levels)
        dx, dy = thick * slope_x, thick * slope_y
        gu, gv = spread_out(k_pu[k] * dx, k_b[k] * dx, k_pv[k] * dx, k_qv[k] * dy, k_c[k] * dy, k_qu[k] * dy)
        gu_ref[k] = gu_ref[k] + gu + k_u[k] * dx[:ROWS, :COLS]
        gv_ref[k] = gv_ref[k] + gv + k_v[k] * dy[:ROWS, :COLS]
        return carry

    lax.fori_loop(0, levels, finish, 0)

    for copy in first + second + third:
        copy.wait_send()
    for i in range(2):
        drain(i, tx_copy, c, n_tx)
        drain(i, ty_copy, r, n_ty)


def on_device(n_ty, n_tx, u, v, t, count, us, vs, ts, elevation):
    levels = u.shape[0]
    block = jax.ShapeDtypeStruct(u.shape, jnp.float32)
    f32 = jnp.float32
    wide = pltpu.VMEM((levels, 2 * ROWS, 2 * COLS), f32)
    own = pltpu.VMEM((levels, ROWS, COLS), f32)
    two = pltpu.VMEM((levels, 2, COLS), f32)
    return pl.pallas_call(
        functools.partial(kernel, levels, n_ty, n_tx),
        out_shape=(block, block, block, jax.ShapeDtypeStruct(elevation.shape, f32)),
        in_specs=[pl.BlockSpec(memory_space=pltpu.VMEM)] * 8,
        out_specs=[pl.BlockSpec(memory_space=pltpu.VMEM)] * 4,
        scratch_shapes=[
            pltpu.VMEM((8, ROWS, COLS), jnp.int32),
            pltpu.VMEM((8, ROWS, COLS), f32),
            pltpu.VMEM((2, ROWS, COLS), f32),
            pltpu.VMEM((8, 2, ROWS, COLS), f32),
            pltpu.VMEM((6, ROWS, COLS), f32),
            pltpu.VMEM((6, 6, ROWS, COLS), f32),
            own, own, two, two,
            own, own, two, two,
            pltpu.VMEM((6, ROWS, COLS), f32),
            pltpu.VMEM((4, ROWS, COLS), f32),
            pltpu.VMEM((4, 1, COLS), f32),
            pltpu.VMEM((2, n_tx, 1, COLS), f32),
            pltpu.VMEM((2, n_ty, 1, COLS), f32),
            wide, wide, wide, wide, wide, wide, own, own,
            pltpu.SemaphoreType.DMA((34,)),
            pltpu.SemaphoreType.DMA((34,)),
            pltpu.SemaphoreType.DMA((2, n_tx)),
            pltpu.SemaphoreType.DMA((2, n_tx)),
            pltpu.SemaphoreType.DMA((2, n_ty)),
            pltpu.SemaphoreType.DMA((2, n_ty)),
        ],
        compiler_params=pltpu.CompilerParams(
            collective_id=0, has_side_effects=True, vmem_limit_bytes=32 * 1024 * 1024
        ),
    )(u, v, t, count, us, vs, ts, elevation)


def solution(mesh):
    field, surface = P(None, "ty", "tx"), P("ty", "tx")
    return jax.shard_map(
        functools.partial(on_device, mesh.shape["ty"], mesh.shape["tx"]),
        mesh=mesh,
        in_specs=(field, field, field, surface, field, field, field, surface),
        out_specs=(field, field, field, surface),
        check_vma=False,
    )
```

```python
import functools

import jax
import jax.numpy as jnp
from jax import lax
from jax.experimental import pallas as pl
from jax.experimental.pallas import tpu as pltpu
from jax.sharding import PartitionSpec as P

MESH = pl.DeviceIdType.MESH
ADVECT = 0.1
GRAVITY_DT = 0.1
ROWS, COLS = 8, 128

E, W, N, S, NE, NW, SE, SW = range(8)
WAY = ((0, 1), (0, -1), (1, 0), (-1, 0), (1, 1), (1, -1), (-1, 1), (-1, -1))
OPPOSITE = (W, E, S, N, SW, SE, NW, NE)

def turn(x, shift, axis):
    return pltpu.roll(x, shift % x.shape[axis], axis)


def east(x):
    return turn(x, -1, 1)


def west(x):
    return turn(x, 1, 1)


def north(x):
    return turn(x, -1, 0)


def south(x):
    return turn(x, 1, 0)


def tile(a, b, c, d):
    return jnp.concatenate(
        [jnp.concatenate([a, b], axis=1), jnp.concatenate([c, d], axis=1)], axis=0
    )


def spread_out(px, pb, pv, qv, qc, qu):
    c1 = qc + north(qc)
    b1 = pb + south(pb)
    gu = 0.5 * (east(px) - west(px) + north(pv) - south(pv)) + 0.25 * (c1 + west(c1))
    gv = 0.5 * (north(qv) - south(qv) + east(qu) - west(qu)) + 0.25 * (b1 + east(b1))
    return gu[:ROWS, :COLS], gv[:ROWS, :COLS]


def kernel(
    levels, n_ty, n_tx,
    u_hbm, v_hbm, t_hbm, count_hbm, us_hbm, vs_hbm, ts_hbm, elev_hbm,
    gu_ref, gv_ref, gt_ref, eta_ref, slope_ref,
    k_pu, k_pv, k_b, k_qv, k_qu, k_c, k_u, k_v,
    u_ref, v_ref, t_ref, us_ref, vs_ref, ts_ref, count_ref, elev_ref,
    count_in, elev_in, col_out, col_in,
    colp_out, colp_in, corner_in, rown_out, rows_out, rown2_out, rows2_out, row_in, row2_in,
    sides, corners, mine, tx_in, ty_in,
    load_sem, send_sem, recv_sem,
):
    r, c = lax.axis_index("ty"), lax.axis_index("tx")
    total_rows = ROWS * n_ty

    def at(d):
        dy, dx = WAY[d]
        return (lax.rem(r + dy + n_ty, n_ty), lax.rem(c + dx + n_tx, n_tx))

    def hop(number, src, dst, d):
        return pltpu.make_async_remote_copy(
            src_ref=src, dst_ref=dst,
            send_sem=send_sem.at[number], recv_sem=recv_sem.at[number],
            device_id=at(d), device_id_type=MESH,
        )

    def whole(number, ref):
        return hop(number, ref, ref, E)

    def fetch(i, src, dst):
        copy = pltpu.make_async_copy(src, dst, load_sem.at[i])
        copy.start()
        return copy

    fetches = [
        fetch(0, u_hbm, u_ref), fetch(1, v_hbm, v_ref), fetch(2, us_hbm, us_ref), fetch(3, vs_hbm, vs_ref),
        fetch(4, t_hbm, t_ref), fetch(5, ts_hbm, ts_ref), fetch(6, count_hbm, count_ref),
        fetch(7, elev_hbm, elev_ref),
    ]
    tx_order = sorted(range(1, n_tx), key=lambda o: -min(o, n_tx - o))
    ty_order = sorted(range(1, n_ty), key=lambda o: -(min(o % 8, 8 - o % 8) + min(o // 8, n_ty // 8 - o // 8)))

    barrier = pltpu.get_barrier_semaphore()

    for o in ty_order:
        pl.semaphore_signal(barrier, inc=1, device_id=(lax.rem(r + o, n_ty), c), device_id_type=MESH)
    for o in tx_order:
        pl.semaphore_signal(barrier, inc=1, device_id=(r, lax.rem(c + o, n_tx)), device_id_type=MESH)
    for d in (NE, NW, SE, SW):
        pl.semaphore_signal(barrier, inc=1, device_id=at(d), device_id_type=MESH)

    lane = lax.broadcasted_iota(jnp.int32, (ROWS, COLS), 1)
    sub = lax.broadcasted_iota(jnp.int32, (ROWS, COLS), 0)
    fields = (u_ref, v_ref, us_ref, vs_ref, t_ref, ts_ref)

    for copy in fetches:
        copy.wait()

    def pack(k, packed):
        x = [f[k] for f in fields]
        here = lax.div(lane, 4) == k
        shift = lax.rem(4 * k + 2, COLS)
        packed = tuple(jnp.where(here, pltpu.roll(a, shift, 1), b) for a, b in zip(x, packed))
        u, v, us, vs, t, ts = x
        rown_out[k] = jnp.where(
            sub >= 6, u, jnp.where(sub >= 4, turn(v, -2, 0), jnp.where(sub >= 2, turn(t, 4, 0), turn(ts, 2, 0)))
        )
        rows_out[k] = jnp.where(
            sub < 2, u, jnp.where(sub < 4, turn(v, 2, 0), jnp.where(sub < 6, turn(t, 4, 0), turn(ts, -2, 0)))
        )
        rown2_out[k] = jnp.concatenate([us[7:8], vs[7:8]], axis=0)
        rows2_out[k] = jnp.concatenate([us[0:1], vs[0:1]], axis=0)
        return packed

    packed = lax.fori_loop(0, levels, pack, tuple(jnp.zeros((ROWS, COLS), jnp.float32) for _ in fields))
    for f in range(6):
        colp_out[f] = packed[f]

    pl.semaphore_wait(barrier, (n_tx - 1) + (n_ty - 1) + 4)

    for d in range(8):
        hop(0, count_ref, count_in.at[OPPOSITE[d]], d).start()
        hop(1, elev_ref, elev_in.at[OPPOSITE[d]], d).start()

    wide_row = lax.broadcasted_iota(jnp.int32, (3 * ROWS, 2 * COLS), 0)
    wide_col = lax.broadcasted_iota(jnp.int32, (3 * ROWS, 2 * COLS), 1)
    row_at = r * ROWS + jnp.where(wide_row < 16, wide_row, wide_row - 24)
    col_at = c * COLS + jnp.where(wide_col < 192, wide_col, wide_col - 256)
    inside = (row_at >= 0) & (row_at < total_rows) & (col_at >= 0) & (col_at < COLS * n_tx)

    def around(own, part):
        rim = [jnp.where(lane < 64, part(a), part(b)) for a, b in ((E, W), (NE, NW), (SE, SW))]
        return jnp.concatenate(
            [jnp.concatenate([a, b], axis=1) for a, b in zip((own, part(N), part(S)), rim)], axis=0
        )

    whole(0, count_in).wait_recv()
    whole(1, elev_in).wait_recv()
    count = jnp.where(inside, around(count_ref[...], lambda d: count_in[d]).astype(jnp.float32), 0.0)
    count_u = jnp.minimum(count, west(count))
    count_v = jnp.minimum(count, south(count))
    depth_u = count_u + count_u * (count_u - 1.0) * (0.5 / levels)
    depth_v = count_v + count_v * (count_v - 1.0) * (0.5 / levels)

    own_u, own_v = count_u[:ROWS, :COLS], count_v[:ROWS, :COLS]
    col_u = jnp.zeros((ROWS, COLS), jnp.float32)
    col_v = jnp.zeros((ROWS, COLS), jnp.float32)
    for k in range(levels):
        col_u = col_u + jnp.where(own_u > float(k), us_ref[k], 0.0)
        col_v = col_v + jnp.where(own_v > float(k), vs_ref[k], 0.0)
    col_out[0] = col_u
    col_out[1] = col_v
    for d in range(8):
        hop(2, col_out, col_in.at[OPPOSITE[d]], d).start()

    hop(3, rown_out, row_in.at[1], N).start()
    hop(3, rows_out, row_in.at[0], S).start()
    hop(4, rown2_out, row2_in.at[1], N).start()
    hop(4, rows2_out, row2_in.at[0], S).start()
    for d in (E, W):
        hop(5, colp_out, colp_in.at[OPPOSITE[d]], d).start()
    for d in (NE, NW, SE, SW):
        hop(6, colp_out.at[0:4], corner_in.at[OPPOSITE[d] - NE], d).start()

    def squeeze(x):
        low = lax.broadcasted_iota(jnp.int32, (ROWS, 2 * COLS), 0) < 4
        return jnp.concatenate([x[:ROWS], jnp.where(low, x[ROWS : 2 * ROWS], x[2 * ROWS :])], axis=0)

    cu, cv = squeeze(count_u), squeeze(count_v)
    row16 = lax.broadcasted_iota(jnp.int32, (2 * ROWS, 2 * COLS), 0)
    row16 = (r * ROWS + jnp.where(row16 < 12, row16, row16 - 16)).astype(jnp.float32)
    fu = 0.5 + (row16 + 0.5) / total_rows
    fv = 0.5 + row16 / total_rows

    whole(2, col_in).wait_recv()
    col_u = jnp.where(inside, around(col_out[0], lambda d: col_in[d, 0]), 0.0)
    col_v = jnp.where(inside, around(col_out[1], lambda d: col_in[d, 1]), 0.0)
    elevation = around(elev_ref[...], lambda d: elev_in[d])
    load = jnp.where(
        inside, elevation + GRAVITY_DT * (east(col_u) - col_u + north(col_v) - col_v), 0.0
    )

    def operate(p):
        flow_u = depth_u * (p - west(p))
        flow_v = depth_v * (p - south(p))
        return p - GRAVITY_DT * (east(flow_u) - flow_u + north(flow_v) - flow_v)

    sub16 = lax.broadcasted_iota(jnp.int32, (16, COLS), 0)
    lane16 = lax.broadcasted_iota(jnp.int32, (16, COLS), 1)
    lane1 = lax.broadcasted_iota(jnp.int32, (1, COLS), 1)

    def dots(pairs):
        sums = jnp.zeros((16, COLS), jnp.float32)
        for m, (a, b) in enumerate(pairs):
            part = jnp.sum(a[:ROWS, :COLS] * b[:ROWS, :COLS], axis=0, keepdims=True)
            sums = jnp.where(sub16 == m, part, sums)
        sums = jnp.sum(sums, axis=1, keepdims=True)
        return jnp.sum(jnp.where(lane16 == sub16, sums, 0.0), axis=0, keepdims=True)

    def tx_copy(i, o):
        return pltpu.make_async_remote_copy(
            src_ref=mine.at[2 * i], dst_ref=tx_in.at[i, o - 1],
            send_sem=send_sem.at[7 + i], recv_sem=recv_sem.at[7 + i],
            device_id=(r, lax.rem(c + o, n_tx)), device_id_type=MESH,
        )

    def ty_copy(i, o):
        return pltpu.make_async_remote_copy(
            src_ref=mine.at[2 * i + 1], dst_ref=ty_in.at[i, o - 1],
            send_sem=send_sem.at[9 + i], recv_sem=recv_sem.at[9 + i],
            device_id=(lax.rem(r + o, n_ty), c), device_id_type=MESH,
        )

    def total(i, row, cover_tx, cover_ty):
        mine[2 * i] = row
        for o in tx_order:
            tx_copy(i, o).start()
        cover_tx()
        whole(7 + i, tx_in.at[i]).wait_recv()
        row = row + jnp.sum(tx_in[i], axis=0)
        mine[2 * i + 1] = row
        for o in ty_order:
            ty_copy(i, o).start()
        cover_ty()
        whole(9 + i, ty_in.at[i]).wait_recv()
        return row + jnp.sum(ty_in[i], axis=0)

    def pick(row, m):
        return jnp.sum(jnp.where(lane1 == m, row, 0.0), axis=1, keepdims=True)

    inner = lax.rem(lane, 4) < 2
    low8 = sub < 4
    beside = jnp.where(inner, c, n_tx - 1 - c) > 0
    beyond = jnp.where(low8, n_ty - 1 - r, r) > 0

    def receive():
        for number, ref in ((3, row_in), (4, row2_in), (5, colp_in), (6, corner_in)):
            whole(number, ref).wait_recv()
        for f in range(6):
            side = jnp.where(inner, colp_in[W, f], colp_in[E, f])
            sides[f] = jnp.where(beside, side, 0.0)
        for f in range(4):
            upper = jnp.where(inner, corner_in[NW - NE, f], corner_in[NE - NE, f])
            lower = jnp.where(inner, corner_in[SW - NE, f], corner_in[SE - NE, f])
            corners[f] = jnp.where(beside & beyond, jnp.where(low8, upper, lower), 0.0)

    def prepare(k, carry):
        shift = lax.rem(126 - 4 * k + COLS, COLS)
        nb, sb = row_in[0, k], row_in[1, k]
        nb2, sb2 = row2_in[0, k], row2_in[1, k]

        def wide(f, ref, ends):
            side = pltpu.roll(sides[f], shift, 1)
            corner = pltpu.roll(corners[f], shift, 1) if f < 4 else side
            return tile(ref[k], side, jnp.where(beyond, ends, 0.0), corner)

        def both(f, ref):
            i = f - 2
            ends = jnp.where(
                low8,
                jnp.broadcast_to(nb2[i : i + 1], (ROWS, COLS)),
                jnp.broadcast_to(sb2[i : i + 1], (ROWS, COLS)),
            )
            return wide(f, ref, ends)

        u = wide(0, u_ref, jnp.where(low8, nb, sb))
        v = wide(1, v_ref, jnp.where(low8, turn(nb, -2, 0), turn(sb, 2, 0)))
        t = wide(4, t_ref, jnp.where(low8, turn(nb, 4, 0), turn(sb, 4, 0)))
        ts = wide(5, ts_ref, jnp.where(low8, turn(nb, 2, 0), turn(sb, -2, 0)))
        us = both(2, us_ref)
        vs = both(3, vs_ref)
        level = k.astype(jnp.float32)
        mask_u = jnp.where(cu > level, ADVECT, 0.0)
        mask_v = jnp.where(cv > level, ADVECT, 0.0)

        flux_x = mask_u * (ts - west(ts))
        flux_y = mask_v * (ts - south(ts))
        x, y = u * flux_x, v * flux_y
        xe, yn = east(x), north(y)
        gt = ts + (
            7.0 * (x + xe + y + yn) - (west(x) + east(xe) + south(y) + north(yn))
        ) * (1.0 / 12.0)
        gt_ref[k] = gt[:ROWS, :COLS]
        tw, tso = west(t), south(t)
        face_x = (7.0 * (t + tw) - (east(t) + west(tw))) * (1.0 / 12.0)
        face_y = (7.0 * (t + tso) - (north(t) + south(tso))) * (1.0 / 12.0)

        ue, vn = east(u), north(v)
        pair_v, pair_u = v + vn, u + ue
        v_bar = 0.25 * (pair_v + west(pair_v))
        u_bar = 0.25 * (pair_u + south(pair_u))
        kpu = mask_u * u
        kpv = mask_u * v_bar
        kb = mask_u * (fu - 0.5 * (north(u) - south(u)))
        kqv = mask_v * v
        kqu = mask_v * u_bar
        kc = -mask_v * (fv + 0.5 * (east(v) - west(v)))
        k_pu[k], k_pv[k], k_b[k] = kpu, kpv, kb
        k_qv[k], k_qu[k], k_c[k] = kqv, kqu, kc
        own_mu, own_mv = mask_u[:ROWS, :COLS], mask_v[:ROWS, :COLS]
        ku = -0.5 * own_mu * (ue - west(u))[:ROWS, :COLS]
        kv = -0.5 * own_mv * (vn - south(v))[:ROWS, :COLS]
        k_u[k] = ku + jnp.where(own_mu > 0.0, 1.0, 0.0)
        k_v[k] = kv + jnp.where(own_mv > 0.0, 1.0, 0.0)
        gu, gv = spread_out(kpu * us, kb * us, kpv * us, kqv * vs, kc * vs, kqu * vs)
        own_us, own_vs = us_ref[k], vs_ref[k]
        gu_ref[k] = gu + own_us + own_us * ku + (flux_x * face_x)[:ROWS, :COLS]
        gv_ref[k] = gv + own_vs + own_vs * kv + (flux_y * face_y)[:ROWS, :COLS]
        return carry

    third_of = levels // 3

    def cover_first():
        receive()
        lax.fori_loop(0, third_of, prepare, 0)

    p0 = load
    p1 = operate(p0)
    p2 = operate(p1)
    row = total(
        0, dots([(p0, p0), (p0, p1), (p1, p1), (p1, p2)]), lambda: None, cover_first
    )
    g00, g01, g11, g12 = [pick(row, m) for m in range(4)]
    alpha1 = g00 / g01
    norm1 = g00 - 2.0 * alpha1 * g01 + alpha1 * alpha1 * g11
    beta1 = norm1 / g00
    e0, e1 = 1.0 + beta1, -alpha1
    alpha2 = norm1 / (e0 * e0 * g01 + 2.0 * e0 * e1 * g11 + e1 * e1 * g12)
    d1 = e0 * p0 + e1 * p1
    x2 = alpha1 * p0 + alpha2 * d1
    w0 = (p0 - alpha1 * p1) - alpha2 * (e0 * p1 + e1 * p2)

    w1 = d1
    w2, w3 = operate(w0), operate(w1)
    w4, w5 = operate(w2), operate(w3)
    row = total(
        1,
        dots(
            [(w0, w0), (w0, w2), (w0, w3), (w1, w3), (w2, w2), (w2, w3), (w3, w3), (w2, w4), (w2, w5), (w3, w5)]
        ),
        lambda: lax.fori_loop(third_of, 2 * third_of, prepare, 0),
        lambda: lax.fori_loop(2 * third_of, levels, prepare, 0),
    )
    h00, h02, h03, h13, h22, h23, h33, h24, h25, h35 = [pick(row, m) for m in range(10)]
    beta2 = h00 / norm1
    twice, square = 2.0 * beta2, beta2 * beta2
    d_a_d = h02 + twice * h03 + square * h13
    ad_ad = h22 + twice * h23 + square * h33
    d_aaa_d = h24 + twice * h25 + square * h35
    r_a_d = h02 + beta2 * h03
    ar_ad = h22 + beta2 * h23
    alpha3 = h00 / d_a_d
    norm3 = h00 - 2.0 * alpha3 * r_a_d + alpha3 * alpha3 * ad_ad
    beta3 = norm3 / h00
    alpha4 = norm3 / (
        h02 + 2.0 * beta3 * r_a_d - 2.0 * alpha3 * ar_ad
        + beta3 * beta3 * d_a_d - 2.0 * alpha3 * beta3 * ad_ad + alpha3 * alpha3 * d_aaa_d
    )
    d2 = w0 + beta2 * w1
    d3 = w0 + beta3 * d2 - alpha3 * (w2 + beta2 * w3)
    answer = x2 + alpha3 * d2 + alpha4 * d3
    eta_ref[...] = answer[:ROWS, :COLS]
    slope_ref[0] = squeeze(answer - west(answer))
    slope_ref[1] = squeeze(answer - south(answer))

    for number, ref in (
        (0, count_in), (1, elev_in), (2, col_in), (3, row_in), (4, row2_in), (5, colp_in), (6, corner_in),
        (7, tx_in.at[0]), (8, tx_in.at[1]), (9, ty_in.at[0]), (10, ty_in.at[1]),
    ):
        whole(number, ref).wait_send()


def finish(
    levels, pieces,
    gu_ref, gv_ref, gt_ref, eta_ref, slope_ref, k_pu, k_pv, k_b, k_qv, k_qu, k_c, k_u, k_v,
    gu_hbm, gv_hbm, gt_hbm, eta_hbm,
    gu_out, gv_out, sems,
):
    copies = [
        pltpu.make_async_copy(gt_ref, gt_hbm, sems.at[0]),
        pltpu.make_async_copy(eta_ref, eta_hbm, sems.at[1]),
    ]
    for copy in copies:
        copy.start()
    slope_x, slope_y = slope_ref[0], slope_ref[1]

    def level(k, carry):
        thick = 1.0 + k.astype(jnp.float32) * (1.0 / levels)
        dx, dy = thick * slope_x, thick * slope_y
        gu, gv = spread_out(k_pu[k] * dx, k_b[k] * dx, k_pv[k] * dx, k_qv[k] * dy, k_c[k] * dy, k_qu[k] * dy)
        gu_out[k] = gu_ref[k] + gu + k_u[k] * dx[:ROWS, :COLS]
        gv_out[k] = gv_ref[k] + gv + k_v[k] * dy[:ROWS, :COLS]
        return carry

    size = levels // pieces
    for i in range(pieces):
        lax.fori_loop(i * size, (i + 1) * size, level, 0)
        part = pl.ds(i * size, size)
        for g, (src, dst) in enumerate(((gu_out, gu_hbm), (gv_out, gv_hbm))):
            copy = pltpu.make_async_copy(src.at[part], dst.at[part], sems.at[2 + 2 * i + g])
            copy.start()
            copies.append(copy)
    for copy in copies:
        copy.wait()


def on_device(n_ty, n_tx, u, v, t, count, us, vs, ts, elevation):
    levels = u.shape[0]
    f32 = jnp.float32
    block = jax.ShapeDtypeStruct(u.shape, f32)
    face = jax.ShapeDtypeStruct(elevation.shape, f32)
    around = jax.ShapeDtypeStruct((levels, 2 * ROWS, 2 * COLS), f32)
    slopes = jax.ShapeDtypeStruct((2, 2 * ROWS, 2 * COLS), f32)
    own = pltpu.VMEM((levels, ROWS, COLS), f32)
    two = pltpu.VMEM((levels, 2, COLS), f32)
    tiles = lambda *n, dtype=f32: pltpu.VMEM((*n, ROWS, COLS), dtype)
    vmem, hbm = pl.BlockSpec(memory_space=pltpu.VMEM), pl.BlockSpec(memory_space=pltpu.HBM)
    parts = pl.pallas_call(
        functools.partial(kernel, levels, n_ty, n_tx),
        out_shape=(block, block, block, face, slopes) + (around,) * 6 + (block, block),
        in_specs=[hbm] * 8,
        out_specs=[vmem] * 13,
        scratch_shapes=[
            own, own, own, own, own, own, tiles(dtype=jnp.int32), tiles(),
            tiles(8, dtype=jnp.int32), tiles(8), tiles(2), tiles(8, 2),
            tiles(6), tiles(2, 6), tiles(4, 4), own, own, two, two,
            tiles(2, levels), pltpu.VMEM((2, levels, 2, COLS), f32),
            tiles(6), tiles(4),
            pltpu.VMEM((4, 1, COLS), f32),
            pltpu.VMEM((2, n_tx - 1, 1, COLS), f32),
            pltpu.VMEM((2, n_ty - 1, 1, COLS), f32),
            pltpu.SemaphoreType.DMA((8,)),
            pltpu.SemaphoreType.DMA((11,)),
            pltpu.SemaphoreType.DMA((11,)),
        ],
        compiler_params=pltpu.CompilerParams(
            collective_id=0, has_side_effects=True, vmem_limit_bytes=32 * 1024 * 1024
        ),
    )(*[pltpu.with_memory_space_constraint(x, pltpu.HBM) for x in (u, v, t, count, us, vs, ts, elevation)])
    pieces = 3
    return pl.pallas_call(
        functools.partial(finish, levels, pieces),
        out_shape=(block, block, block, face),
        in_specs=[vmem] * 13,
        out_specs=[hbm] * 4,
        scratch_shapes=[own, own, pltpu.SemaphoreType.DMA((2 + 2 * pieces,))],
        compiler_params=pltpu.CompilerParams(vmem_limit_bytes=16 * 1024 * 1024),
    )(*parts)


def solution(mesh):
    field, surface = P(None, "ty", "tx"), P("ty", "tx")
    return jax.shard_map(
        functools.partial(on_device, mesh.shape["ty"], mesh.shape["tx"]),
        mesh=mesh,
        in_specs=(field, field, field, surface, field, field, field, surface),
        out_specs=(field, field, field, surface),
        check_vma=False,
    )
```

```python
import functools

import jax
import jax.numpy as jnp
from jax import lax
from jax.experimental import pallas as pl
from jax.experimental.pallas import tpu as pltpu
from jax.sharding import PartitionSpec as P

MESH = pl.DeviceIdType.MESH
ADVECT = 0.1
GRAVITY_DT = 0.1
ROWS, COLS = 8, 128

W, S, E, N, NE, NW, SE, SW = range(8)
WAY = ((0, -1), (-1, 0), (0, 1), (1, 0), (1, 1), (1, -1), (-1, 1), (-1, -1))
OPPOSITE = (E, N, W, S, SW, SE, NW, NE)


def turn(x, shift, axis):
    return pltpu.roll(x, shift % x.shape[axis], axis)


def east(x):
    return turn(x, -1, 1)


def west(x):
    return turn(x, 1, 1)


def north(x):
    return turn(x, -1, 0)


def south(x):
    return turn(x, 1, 0)


def tile(a, b, c, d):
    return jnp.concatenate(
        [jnp.concatenate([a, b], axis=1), jnp.concatenate([c, d], axis=1)], axis=0
    )


CROSS = ((0, 0), (0, 1), (0, -1), (1, 0), (-1, 0))
U_CORNERS = ((0, 0), (0, -1), (1, 0), (1, -1))
V_CORNERS = ((0, 0), (0, 1), (-1, 0), (-1, 1))


def seen(x, place):
    dy, dx = place
    x = turn(x, -dx, 1) if dx else x
    x = turn(x, -dy, 0) if dy else x
    return x[:ROWS, :COLS]


def gather(weights, values):
    total = weights[0] * values[0]
    for a, b in zip(weights[1:], values[1:]):
        total = total + a * b
    return total


def kernel(
    levels, n_ty, n_tx,
    u_hbm, v_hbm, t_hbm, count_hbm, us_hbm, vs_hbm, ts_hbm, elev_hbm,
    gu_ref, gv_ref, gt_ref, eta_ref, slope_ref,
    u_weights, v_weights,
    u_ref, v_ref, t_ref, us_ref, vs_ref, ts_ref, count_ref, elev_ref,
    count_in, elev_in, col_out, col_in,
    colp_out, colp_in, corner_in, rown_out, rows_out, rown2_out, rows2_out, row_in, row2_in,
    sides, corners, mine, tx_in, ty_in,
    load_sem, send_sem, recv_sem,
):
    r, c = lax.axis_index("ty"), lax.axis_index("tx")
    total_rows = ROWS * n_ty

    def at(d):
        dy, dx = WAY[d]
        return (lax.rem(r + dy + n_ty, n_ty), lax.rem(c + dx + n_tx, n_tx))

    def hop(number, src, dst, d):
        return pltpu.make_async_remote_copy(
            src_ref=src, dst_ref=dst,
            send_sem=send_sem.at[number], recv_sem=recv_sem.at[number],
            device_id=at(d), device_id_type=MESH,
        )

    def whole(number, ref):
        return hop(number, ref, ref, E)

    def fetch(i, src, dst):
        copy = pltpu.make_async_copy(src, dst, load_sem.at[i])
        copy.start()
        return copy

    fetches = [
        fetch(0, u_hbm, u_ref), fetch(1, v_hbm, v_ref), fetch(2, us_hbm, us_ref), fetch(3, vs_hbm, vs_ref),
        fetch(4, t_hbm, t_ref), fetch(5, ts_hbm, ts_ref), fetch(6, count_hbm, count_ref),
        fetch(7, elev_hbm, elev_ref),
    ]
    tx_order = sorted(range(1, n_tx), key=lambda o: -min(o, n_tx - o))
    ty_order = sorted(range(1, n_ty), key=lambda o: -(min(o % 8, 8 - o % 8) + min(o // 8, n_ty // 8 - o // 8)))

    barrier = pltpu.get_barrier_semaphore()

    for o in ty_order:
        pl.semaphore_signal(barrier, inc=1, device_id=(lax.rem(r + o, n_ty), c), device_id_type=MESH)
    for o in tx_order:
        pl.semaphore_signal(barrier, inc=1, device_id=(r, lax.rem(c + o, n_tx)), device_id_type=MESH)
    for d in (NE, NW, SE, SW):
        pl.semaphore_signal(barrier, inc=1, device_id=at(d), device_id_type=MESH)

    lane = lax.broadcasted_iota(jnp.int32, (ROWS, COLS), 1)
    sub = lax.broadcasted_iota(jnp.int32, (ROWS, COLS), 0)
    fields = (u_ref, v_ref, us_ref, vs_ref, t_ref, ts_ref)

    for copy in fetches:
        copy.wait()

    def pack(k, packed):
        x = [f[k] for f in fields]
        here = lax.div(lane, 4) == k
        shift = lax.rem(4 * k + 2, COLS)
        packed = tuple(jnp.where(here, pltpu.roll(a, shift, 1), b) for a, b in zip(x, packed))
        u, v, us, vs, t, ts = x
        rown_out[k] = jnp.where(
            sub >= 6, u, jnp.where(sub >= 4, turn(v, -2, 0), jnp.where(sub >= 2, turn(t, 4, 0), turn(ts, 2, 0)))
        )
        rows_out[k] = jnp.where(
            sub < 2, u, jnp.where(sub < 4, turn(v, 2, 0), jnp.where(sub < 6, turn(t, 4, 0), turn(ts, -2, 0)))
        )
        rown2_out[k] = jnp.concatenate([us[7:8], vs[7:8]], axis=0)
        rows2_out[k] = jnp.concatenate([us[0:1], vs[0:1]], axis=0)
        return packed

    packed = lax.fori_loop(0, levels, pack, tuple(jnp.zeros((ROWS, COLS), jnp.float32) for _ in fields))
    for f in range(6):
        colp_out[f] = packed[f]

    pl.semaphore_wait(barrier, (n_tx - 1) + (n_ty - 1) + 4)

    for d in (N, E):
        hop(0, count_ref, count_in.at[OPPOSITE[d]], d).start()
    for d in (NE, NW, SE, SW, S, W):
        hop(11, count_ref, count_in.at[OPPOSITE[d]], d).start()
    for d in (NE, NW, SE, SW, S, W, N, E):
        hop(1, elev_ref, elev_in.at[OPPOSITE[d]], d).start()

    wide_row = lax.broadcasted_iota(jnp.int32, (3 * ROWS, 2 * COLS), 0)
    wide_col = lax.broadcasted_iota(jnp.int32, (3 * ROWS, 2 * COLS), 1)
    row_at = r * ROWS + jnp.where(wide_row < 16, wide_row, wide_row - 24)
    col_at = c * COLS + jnp.where(wide_col < 192, wide_col, wide_col - 256)
    inside = (row_at >= 0) & (row_at < total_rows) & (col_at >= 0) & (col_at < COLS * n_tx)

    def around(own, part):
        rim = [jnp.where(lane < 64, part(a), part(b)) for a, b in ((E, W), (NE, NW), (SE, SW))]
        return jnp.concatenate(
            [jnp.concatenate([a, b], axis=1) for a, b in zip((own, part(N), part(S)), rim)], axis=0
        )

    whole(0, count_in.at[0:2]).wait_recv()
    own_count = count_ref[...]
    own_u = jnp.minimum(own_count, jnp.where(lane == 0, west(count_in[W]), west(own_count))).astype(jnp.float32)
    own_v = jnp.minimum(own_count, jnp.where(sub == 0, south(count_in[S]), south(own_count))).astype(jnp.float32)
    own_u = jnp.where((lane == 0) & (c == 0), 0.0, own_u)
    own_v = jnp.where((sub == 0) & (r == 0), 0.0, own_v)
    col_u = jnp.zeros((ROWS, COLS), jnp.float32)
    col_v = jnp.zeros((ROWS, COLS), jnp.float32)
    for k in range(levels):
        col_u = col_u + jnp.where(own_u > float(k), us_ref[k], 0.0)
        col_v = col_v + jnp.where(own_v > float(k), vs_ref[k], 0.0)
    col_out[0] = col_u
    col_out[1] = col_v
    for d in (NE, NW, SE, SW, N, S, E, W):
        hop(2, col_out, col_in.at[OPPOSITE[d]], d).start()

    hop(3, rown_out, row_in.at[1], N).start()
    hop(3, rows_out, row_in.at[0], S).start()
    hop(4, rown2_out, row2_in.at[1], N).start()
    hop(4, rows2_out, row2_in.at[0], S).start()
    for d in (E, W):
        hop(5, colp_out, colp_in.at[0 if d == E else 1], d).start()
    for d in (NE, NW, SE, SW):
        hop(6, colp_out.at[0:4], corner_in.at[OPPOSITE[d] - NE], d).start()

    def squeeze(x):
        low = lax.broadcasted_iota(jnp.int32, (ROWS, 2 * COLS), 0) < 4
        return jnp.concatenate([x[:ROWS], jnp.where(low, x[ROWS : 2 * ROWS], x[2 * ROWS :])], axis=0)

    whole(11, count_in.at[2:8]).wait_recv()
    whole(1, elev_in).wait_recv()
    count = jnp.where(inside, around(count_ref[...], lambda d: count_in[d]).astype(jnp.float32), 0.0)
    count_u = jnp.minimum(count, west(count))
    count_v = jnp.minimum(count, south(count))
    depth_u = count_u + count_u * (count_u - 1.0) * (0.5 / levels)
    depth_v = count_v + count_v * (count_v - 1.0) * (0.5 / levels)
    cu, cv = squeeze(count_u), squeeze(count_v)
    row16 = lax.broadcasted_iota(jnp.int32, (2 * ROWS, 2 * COLS), 0)
    row16 = (r * ROWS + jnp.where(row16 < 12, row16, row16 - 16)).astype(jnp.float32)
    fu = 0.5 + (row16 + 0.5) / total_rows
    fv = 0.5 + row16 / total_rows

    whole(2, col_in).wait_recv()
    col_u = jnp.where(inside, around(col_out[0], lambda d: col_in[d, 0]), 0.0)
    col_v = jnp.where(inside, around(col_out[1], lambda d: col_in[d, 1]), 0.0)
    elevation = around(elev_ref[...], lambda d: elev_in[d])
    load = jnp.where(
        inside, elevation + GRAVITY_DT * (east(col_u) - col_u + north(col_v) - col_v), 0.0
    )

    def operate(p):
        flow_u = depth_u * (p - west(p))
        flow_v = depth_v * (p - south(p))
        return p - GRAVITY_DT * (east(flow_u) - flow_u + north(flow_v) - flow_v)

    sub16 = lax.broadcasted_iota(jnp.int32, (16, COLS), 0)
    lane16 = lax.broadcasted_iota(jnp.int32, (16, COLS), 1)
    lane1 = lax.broadcasted_iota(jnp.int32, (1, COLS), 1)

    def dots(pairs):
        sums = jnp.zeros((16, COLS), jnp.float32)
        for m, (a, b) in enumerate(pairs):
            part = jnp.sum(a[:ROWS, :COLS] * b[:ROWS, :COLS], axis=0, keepdims=True)
            sums = jnp.where(sub16 == m, part, sums)
        sums = jnp.sum(sums, axis=1, keepdims=True)
        return jnp.sum(jnp.where(lane16 == sub16, sums, 0.0), axis=0, keepdims=True)

    def tx_copy(i, o):
        return pltpu.make_async_remote_copy(
            src_ref=mine.at[2 * i], dst_ref=tx_in.at[i, o - 1],
            send_sem=send_sem.at[7 + i], recv_sem=recv_sem.at[7 + i],
            device_id=(r, lax.rem(c + o, n_tx)), device_id_type=MESH,
        )

    def ty_copy(i, o):
        return pltpu.make_async_remote_copy(
            src_ref=mine.at[2 * i + 1], dst_ref=ty_in.at[i, o - 1],
            send_sem=send_sem.at[9 + i], recv_sem=recv_sem.at[9 + i],
            device_id=(lax.rem(r + o, n_ty), c), device_id_type=MESH,
        )

    def total(i, row, cover_tx, cover_ty):
        mine[2 * i] = row
        for o in tx_order:
            tx_copy(i, o).start()
        cover_tx()
        whole(7 + i, tx_in.at[i]).wait_recv()
        row = row + jnp.sum(tx_in[i], axis=0)
        mine[2 * i + 1] = row
        for o in ty_order:
            ty_copy(i, o).start()
        cover_ty()
        whole(9 + i, ty_in.at[i]).wait_recv()
        return row + jnp.sum(ty_in[i], axis=0)

    def pick(row, m):
        return jnp.sum(jnp.where(lane1 == m, row, 0.0), axis=1, keepdims=True)

    inner = lax.rem(lane, 4) < 2
    low8 = sub < 4
    beside = jnp.where(inner, c, n_tx - 1 - c) > 0
    beyond = jnp.where(low8, n_ty - 1 - r, r) > 0

    def receive():
        for number, ref in ((3, row_in), (4, row2_in), (5, colp_in), (6, corner_in)):
            whole(number, ref).wait_recv()
        for f in range(6):
            side = jnp.where(inner, colp_in[0, f], colp_in[1, f])
            sides[f] = jnp.where(beside, side, 0.0)
        for f in range(4):
            upper = jnp.where(inner, corner_in[NW - NE, f], corner_in[NE - NE, f])
            lower = jnp.where(inner, corner_in[SW - NE, f], corner_in[SE - NE, f])
            corners[f] = jnp.where(beside & beyond, jnp.where(low8, upper, lower), 0.0)

    def prepare(k, carry):
        shift = lax.rem(126 - 4 * k + COLS, COLS)
        nb, sb = row_in[0, k], row_in[1, k]
        nb2, sb2 = row2_in[0, k], row2_in[1, k]

        def wide(f, ref, ends):
            side = pltpu.roll(sides[f], shift, 1)
            corner = pltpu.roll(corners[f], shift, 1) if f < 4 else side
            return tile(ref[k], side, jnp.where(beyond, ends, 0.0), corner)

        def both(f, ref):
            i = f - 2
            ends = jnp.where(
                low8,
                jnp.broadcast_to(nb2[i : i + 1], (ROWS, COLS)),
                jnp.broadcast_to(sb2[i : i + 1], (ROWS, COLS)),
            )
            return wide(f, ref, ends)

        u = wide(0, u_ref, jnp.where(low8, nb, sb))
        v = wide(1, v_ref, jnp.where(low8, turn(nb, -2, 0), turn(sb, 2, 0)))
        t = wide(4, t_ref, jnp.where(low8, turn(nb, 4, 0), turn(sb, 4, 0)))
        ts = wide(5, ts_ref, jnp.where(low8, turn(nb, 2, 0), turn(sb, -2, 0)))
        us = both(2, us_ref)
        vs = both(3, vs_ref)
        level = k.astype(jnp.float32)
        mask_u = jnp.where(cu > level, ADVECT, 0.0)
        mask_v = jnp.where(cv > level, ADVECT, 0.0)

        flux_x = mask_u * (ts - west(ts))
        flux_y = mask_v * (ts - south(ts))
        x, y = u * flux_x, v * flux_y
        xe, yn = east(x), north(y)
        gt = ts + (
            7.0 * (x + xe + y + yn) - (west(x) + east(xe) + south(y) + north(yn))
        ) * (1.0 / 12.0)
        gt_ref[k] = gt[:ROWS, :COLS]
        tw, tso = west(t), south(t)
        face_x = (7.0 * (t + tw) - (east(t) + west(tw))) * (1.0 / 12.0)
        face_y = (7.0 * (t + tso) - (north(t) + south(tso))) * (1.0 / 12.0)

        ue, vn = east(u), north(v)
        pair_v, pair_u = v + vn, u + ue
        v_bar = 0.25 * (pair_v + west(pair_v))
        u_bar = 0.25 * (pair_u + south(pair_u))
        ahead_x = 0.5 * mask_u * u
        ahead_y = 0.5 * mask_u * v_bar
        turning = 0.25 * mask_u * (fu - 0.5 * (north(u) - south(u)))
        own_mu, own_mv = mask_u[:ROWS, :COLS], mask_v[:ROWS, :COLS]
        ku = -0.5 * own_mu * (ue - west(u))[:ROWS, :COLS]
        kv = -0.5 * own_mv * (vn - south(v))[:ROWS, :COLS]
        u_cross = [ku, seen(ahead_x, CROSS[1]), -seen(ahead_x, CROSS[2]), seen(ahead_y, CROSS[3]), -seen(ahead_y, CROSS[4])]
        v_corners = [seen(turning, p) for p in V_CORNERS]
        ahead_y = 0.5 * mask_v * v
        ahead_x = 0.5 * mask_v * u_bar
        turning = -0.25 * mask_v * (fv + 0.5 * (east(v) - west(v)))
        v_cross = [kv, seen(ahead_x, CROSS[1]), -seen(ahead_x, CROSS[2]), seen(ahead_y, CROSS[3]), -seen(ahead_y, CROSS[4])]
        u_corners = [seen(turning, p) for p in U_CORNERS]
        us_at, vs_at = [seen(us, p) for p in CROSS], [seen(vs, p) for p in CROSS]
        gu = gather(u_cross + u_corners, us_at + [seen(vs, p) for p in U_CORNERS])
        gv = gather(v_cross + v_corners, vs_at + [seen(us, p) for p in V_CORNERS])
        gu_ref[k] = gu + us_at[0] + (flux_x * face_x)[:ROWS, :COLS]
        gv_ref[k] = gv + vs_at[0] + (flux_y * face_y)[:ROWS, :COLS]
        u_cross[0] = ku + jnp.where(own_mu > 0.0, 1.0, 0.0)
        v_cross[0] = kv + jnp.where(own_mv > 0.0, 1.0, 0.0)
        for m, weight in enumerate(u_cross + u_corners):
            u_weights[k, m] = weight
        for m, weight in enumerate(v_cross + v_corners):
            v_weights[k, m] = weight
        return carry

    third_of = levels // 3

    def cover_first():
        receive()
        lax.fori_loop(0, third_of, prepare, 0)

    p0 = load
    p1 = operate(p0)
    p2 = operate(p1)
    row = total(
        0, dots([(p0, p0), (p0, p1), (p1, p1), (p1, p2)]), lambda: None, cover_first
    )
    g00, g01, g11, g12 = [pick(row, m) for m in range(4)]
    alpha1 = g00 / g01
    norm1 = g00 - 2.0 * alpha1 * g01 + alpha1 * alpha1 * g11
    beta1 = norm1 / g00
    e0, e1 = 1.0 + beta1, -alpha1
    alpha2 = norm1 / (e0 * e0 * g01 + 2.0 * e0 * e1 * g11 + e1 * e1 * g12)
    d1 = e0 * p0 + e1 * p1
    x2 = alpha1 * p0 + alpha2 * d1
    w0 = (p0 - alpha1 * p1) - alpha2 * (e0 * p1 + e1 * p2)

    w1 = d1
    w2, w3 = operate(w0), operate(w1)
    w4, w5 = operate(w2), operate(w3)
    row = total(
        1,
        dots(
            [(w0, w0), (w0, w2), (w0, w3), (w1, w3), (w2, w2), (w2, w3), (w3, w3), (w2, w4), (w2, w5), (w3, w5)]
        ),
        lambda: lax.fori_loop(third_of, 2 * third_of, prepare, 0),
        lambda: lax.fori_loop(2 * third_of, levels, prepare, 0),
    )
    h00, h02, h03, h13, h22, h23, h33, h24, h25, h35 = [pick(row, m) for m in range(10)]
    beta2 = h00 / norm1
    twice, square = 2.0 * beta2, beta2 * beta2
    d_a_d = h02 + twice * h03 + square * h13
    ad_ad = h22 + twice * h23 + square * h33
    d_aaa_d = h24 + twice * h25 + square * h35
    r_a_d = h02 + beta2 * h03
    ar_ad = h22 + beta2 * h23
    alpha3 = h00 / d_a_d
    norm3 = h00 - 2.0 * alpha3 * r_a_d + alpha3 * alpha3 * ad_ad
    beta3 = norm3 / h00
    alpha4 = norm3 / (
        h02 + 2.0 * beta3 * r_a_d - 2.0 * alpha3 * ar_ad
        + beta3 * beta3 * d_a_d - 2.0 * alpha3 * beta3 * ad_ad + alpha3 * alpha3 * d_aaa_d
    )
    d2 = w0 + beta2 * w1
    d3 = w0 + beta3 * d2 - alpha3 * (w2 + beta2 * w3)
    answer = x2 + alpha3 * d2 + alpha4 * d3
    eta_ref[...] = answer[:ROWS, :COLS]
    slope_x, slope_y = answer - west(answer), answer - south(answer)
    for m, (slope, place) in enumerate(
        [(slope_x, p) for p in CROSS] + [(slope_y, p) for p in U_CORNERS]
        + [(slope_y, p) for p in CROSS] + [(slope_x, p) for p in V_CORNERS]
    ):
        slope_ref[m] = seen(slope, place)

    for number, ref in (
        (0, count_in.at[0:2]), (11, count_in.at[2:8]), (1, elev_in), (2, col_in), (3, row_in), (4, row2_in), (5, colp_in), (6, corner_in),
        (7, tx_in.at[0]), (8, tx_in.at[1]), (9, ty_in.at[0]), (10, ty_in.at[1]),
    ):
        whole(number, ref).wait_send()


def finish(
    levels, pieces,
    gu_ref, gv_ref, gt_ref, eta_ref, slope_ref, u_weights, v_weights,
    gu_hbm, gv_hbm, gt_hbm, eta_hbm,
    gu_out, gv_out, sems,
):
    copies = [
        pltpu.make_async_copy(gt_ref, gt_hbm, sems.at[0]),
        pltpu.make_async_copy(eta_ref, eta_hbm, sems.at[1]),
    ]
    for copy in copies:
        copy.start()
    slopes = [slope_ref[m] for m in range(18)]

    def level(k, carry):
        thick = 1.0 + k.astype(jnp.float32) * (1.0 / levels)
        gu_out[k] = gu_ref[k] + thick * gather([u_weights[k, m] for m in range(9)], slopes[:9])
        gv_out[k] = gv_ref[k] + thick * gather([v_weights[k, m] for m in range(9)], slopes[9:])
        return carry

    size = levels // pieces
    for i in range(pieces):
        lax.fori_loop(i * size, (i + 1) * size, level, 0)
        part = pl.ds(i * size, size)
        for g, (src, dst) in enumerate(((gu_out, gu_hbm), (gv_out, gv_hbm))):
            copy = pltpu.make_async_copy(src.at[part], dst.at[part], sems.at[2 + 2 * i + g])
            copy.start()
            copies.append(copy)
    for copy in copies:
        copy.wait()


def on_device(n_ty, n_tx, u, v, t, count, us, vs, ts, elevation):
    levels = u.shape[0]
    f32 = jnp.float32
    block = jax.ShapeDtypeStruct(u.shape, f32)
    face = jax.ShapeDtypeStruct(elevation.shape, f32)
    weights = jax.ShapeDtypeStruct((levels, 9, ROWS, COLS), f32)
    slopes = jax.ShapeDtypeStruct((18, ROWS, COLS), f32)
    own = pltpu.VMEM((levels, ROWS, COLS), f32)
    two = pltpu.VMEM((levels, 2, COLS), f32)
    tiles = lambda *n, dtype=f32: pltpu.VMEM((*n, ROWS, COLS), dtype)
    vmem, hbm = pl.BlockSpec(memory_space=pltpu.VMEM), pl.BlockSpec(memory_space=pltpu.HBM)
    parts = pl.pallas_call(
        functools.partial(kernel, levels, n_ty, n_tx),
        out_shape=(block, block, block, face, slopes, weights, weights),
        in_specs=[hbm] * 8,
        out_specs=[vmem] * 7,
        scratch_shapes=[
            own, own, own, own, own, own, tiles(dtype=jnp.int32), tiles(),
            tiles(8, dtype=jnp.int32), tiles(8), tiles(2), tiles(8, 2),
            tiles(6), tiles(2, 6), tiles(4, 4), own, own, two, two,
            tiles(2, levels), pltpu.VMEM((2, levels, 2, COLS), f32),
            tiles(6), tiles(4),
            pltpu.VMEM((4, 1, COLS), f32),
            pltpu.VMEM((2, n_tx - 1, 1, COLS), f32),
            pltpu.VMEM((2, n_ty - 1, 1, COLS), f32),
            pltpu.SemaphoreType.DMA((8,)),
            pltpu.SemaphoreType.DMA((12,)),
            pltpu.SemaphoreType.DMA((12,)),
        ],
        compiler_params=pltpu.CompilerParams(
            collective_id=0, has_side_effects=True, vmem_limit_bytes=32 * 1024 * 1024
        ),
    )(*[pltpu.with_memory_space_constraint(x, pltpu.HBM) for x in (u, v, t, count, us, vs, ts, elevation)])
    pieces = 3
    return pl.pallas_call(
        functools.partial(finish, levels, pieces),
        out_shape=(block, block, block, face),
        in_specs=[vmem] * 7,
        out_specs=[hbm] * 4,
        scratch_shapes=[own, own, pltpu.SemaphoreType.DMA((2 + 2 * pieces,))],
        compiler_params=pltpu.CompilerParams(vmem_limit_bytes=16 * 1024 * 1024),
    )(*parts)


def solution(mesh):
    field, surface = P(None, "ty", "tx"), P("ty", "tx")
    return jax.shard_map(
        functools.partial(on_device, mesh.shape["ty"], mesh.shape["tx"]),
        mesh=mesh,
        in_specs=(field, field, field, surface, field, field, field, surface),
        out_specs=(field, field, field, surface),
        check_vma=False,
    )
```

```python
import functools

import jax
import jax.numpy as jnp
from jax import lax
from jax.experimental import pallas as pl
from jax.experimental.pallas import tpu as pltpu
from jax.sharding import PartitionSpec as P

MESH = pl.DeviceIdType.MESH
ADVECT = 0.1
GRAVITY_DT = 0.1
ROWS, COLS = 8, 128

W, S, E, N, NE, NW, SE, SW = range(8)
WAY = ((0, -1), (-1, 0), (0, 1), (1, 0), (1, 1), (1, -1), (-1, 1), (-1, -1))
OPPOSITE = (E, N, W, S, SW, SE, NW, NE)


def turn(x, shift, axis):
    return pltpu.roll(x, shift % x.shape[axis], axis)


def east(x):
    return turn(x, -1, 1)


def west(x):
    return turn(x, 1, 1)


def north(x):
    return turn(x, -1, 0)


def south(x):
    return turn(x, 1, 0)


def tile(a, b, c, d):
    return jnp.concatenate(
        [jnp.concatenate([a, b], axis=1), jnp.concatenate([c, d], axis=1)], axis=0
    )


CROSS = ((0, 0), (0, 1), (0, -1), (1, 0), (-1, 0))
U_CORNERS = ((0, 0), (0, -1), (1, 0), (1, -1))
V_CORNERS = ((0, 0), (0, 1), (-1, 0), (-1, 1))


def seen(x, place):
    dy, dx = place
    x = turn(x, -dx, 1) if dx else x
    x = turn(x, -dy, 0) if dy else x
    return x[:ROWS, :COLS]


def gather(weights, values):
    total = weights[0] * values[0]
    for a, b in zip(weights[1:], values[1:]):
        total = total + a * b
    return total


def kernel(
    levels, n_ty, n_tx,
    u_hbm, v_hbm, t_hbm, count_hbm, us_hbm, vs_hbm, ts_hbm, elev_hbm,
    gu_ref, gv_ref, gt_ref, eta_ref, slope_ref,
    u_weights, v_weights,
    u_ref, v_ref, t_ref, us_ref, vs_ref, ts_ref, count_ref, elev_ref,
    count_in, elev_in, col_out, col_in,
    colp_out, colp_in, corner_in, rown_out, rows_out, rown2_out, rows2_out, row_in, row2_in,
    sides, corners, mine, tx_in, ty_in,
    load_sem, send_sem, recv_sem,
):
    r, c = lax.axis_index("ty"), lax.axis_index("tx")
    total_rows = ROWS * n_ty

    def at(d):
        dy, dx = WAY[d]
        return (lax.rem(r + dy + n_ty, n_ty), lax.rem(c + dx + n_tx, n_tx))

    def hop(number, src, dst, d):
        return pltpu.make_async_remote_copy(
            src_ref=src, dst_ref=dst,
            send_sem=send_sem.at[number], recv_sem=recv_sem.at[number],
            device_id=at(d), device_id_type=MESH,
        )

    def whole(number, ref):
        return hop(number, ref, ref, E)

    def fetch(i, src, dst):
        copy = pltpu.make_async_copy(src, dst, load_sem.at[i])
        copy.start()
        return copy

    fetches = [
        fetch(0, u_hbm, u_ref), fetch(1, v_hbm, v_ref), fetch(2, us_hbm, us_ref), fetch(3, vs_hbm, vs_ref),
        fetch(4, t_hbm, t_ref), fetch(5, ts_hbm, ts_ref), fetch(6, count_hbm, count_ref),
        fetch(7, elev_hbm, elev_ref),
    ]
    tx_order = sorted(range(1, n_tx), key=lambda o: -min(o, n_tx - o))
    ty_order = sorted(range(1, n_ty), key=lambda o: -(min(o % 8, 8 - o % 8) + min(o // 8, n_ty // 8 - o // 8)))

    barrier = pltpu.get_barrier_semaphore()

    for o in ty_order:
        pl.semaphore_signal(barrier, inc=1, device_id=(lax.rem(r + o, n_ty), c), device_id_type=MESH)
    for o in tx_order:
        pl.semaphore_signal(barrier, inc=1, device_id=(r, lax.rem(c + o, n_tx)), device_id_type=MESH)
    for d in (NE, NW, SE, SW):
        pl.semaphore_signal(barrier, inc=1, device_id=at(d), device_id_type=MESH)

    lane = lax.broadcasted_iota(jnp.int32, (ROWS, COLS), 1)
    sub = lax.broadcasted_iota(jnp.int32, (ROWS, COLS), 0)
    fields = (u_ref, v_ref, us_ref, vs_ref, t_ref, ts_ref)

    for copy in fetches:
        copy.wait()

    def pack(k, packed):
        x = [f[k] for f in fields]
        here = lax.div(lane, 4) == k
        shift = lax.rem(4 * k + 2, COLS)
        packed = tuple(jnp.where(here, pltpu.roll(a, shift, 1), b) for a, b in zip(x, packed))
        u, v, us, vs, t, ts = x
        rown_out[k] = jnp.where(
            sub >= 6, u, jnp.where(sub >= 4, turn(v, -2, 0), jnp.where(sub >= 2, turn(t, 4, 0), turn(ts, 2, 0)))
        )
        rows_out[k] = jnp.where(
            sub < 2, u, jnp.where(sub < 4, turn(v, 2, 0), jnp.where(sub < 6, turn(t, 4, 0), turn(ts, -2, 0)))
        )
        rown2_out[k] = jnp.concatenate([us[7:8], vs[7:8]], axis=0)
        rows2_out[k] = jnp.concatenate([us[0:1], vs[0:1]], axis=0)
        return packed

    packed = lax.fori_loop(0, levels, pack, tuple(jnp.zeros((ROWS, COLS), jnp.float32) for _ in fields))
    for f in range(6):
        colp_out[f] = packed[f]

    pl.semaphore_wait(barrier, (n_tx - 1) + (n_ty - 1) + 4)

    for d in (N, E):
        hop(0, count_ref, count_in.at[OPPOSITE[d]], d).start()
    for d in (NE, NW, SE, SW, S, W):
        hop(11, count_ref, count_in.at[OPPOSITE[d]], d).start()
    for d in (NE, NW, SE, SW, S, W, N, E):
        hop(1, elev_ref, elev_in.at[OPPOSITE[d]], d).start()

    wide_row = lax.broadcasted_iota(jnp.int32, (3 * ROWS, 2 * COLS), 0)
    wide_col = lax.broadcasted_iota(jnp.int32, (3 * ROWS, 2 * COLS), 1)
    row_at = r * ROWS + jnp.where(wide_row < 16, wide_row, wide_row - 24)
    col_at = c * COLS + jnp.where(wide_col < 192, wide_col, wide_col - 256)
    inside = (row_at >= 0) & (row_at < total_rows) & (col_at >= 0) & (col_at < COLS * n_tx)

    def around(own, part):
        rim = [jnp.where(lane < 64, part(a), part(b)) for a, b in ((E, W), (NE, NW), (SE, SW))]
        return jnp.concatenate(
            [jnp.concatenate([a, b], axis=1) for a, b in zip((own, part(N), part(S)), rim)], axis=0
        )

    whole(0, count_in.at[0:2]).wait_recv()
    own_count = count_ref[...]
    own_u = jnp.minimum(own_count, jnp.where(lane == 0, west(count_in[W]), west(own_count))).astype(jnp.float32)
    own_v = jnp.minimum(own_count, jnp.where(sub == 0, south(count_in[S]), south(own_count))).astype(jnp.float32)
    own_u = jnp.where((lane == 0) & (c == 0), 0.0, own_u)
    own_v = jnp.where((sub == 0) & (r == 0), 0.0, own_v)
    col_u = jnp.zeros((ROWS, COLS), jnp.float32)
    col_v = jnp.zeros((ROWS, COLS), jnp.float32)
    for k in range(levels):
        col_u = col_u + jnp.where(own_u > float(k), us_ref[k], 0.0)
        col_v = col_v + jnp.where(own_v > float(k), vs_ref[k], 0.0)
    col_out[0] = col_u
    col_out[1] = col_v
    for d in (NE, NW, SE, SW, N, S, E, W):
        hop(2, col_out, col_in.at[OPPOSITE[d]], d).start()

    hop(3, rown_out, row_in.at[1], N).start()
    hop(3, rows_out, row_in.at[0], S).start()
    hop(4, rown2_out, row2_in.at[1], N).start()
    hop(4, rows2_out, row2_in.at[0], S).start()
    for d in (E, W):
        hop(5, colp_out, colp_in.at[0 if d == E else 1], d).start()
    for d in (NE, NW, SE, SW):
        hop(6, colp_out.at[0:4], corner_in.at[OPPOSITE[d] - NE], d).start()

    def squeeze(x):
        low = lax.broadcasted_iota(jnp.int32, (ROWS, 2 * COLS), 0) < 4
        return jnp.concatenate([x[:ROWS], jnp.where(low, x[ROWS : 2 * ROWS], x[2 * ROWS :])], axis=0)

    whole(11, count_in.at[2:8]).wait_recv()
    whole(1, elev_in).wait_recv()
    count = jnp.where(inside, around(count_ref[...], lambda d: count_in[d]).astype(jnp.float32), 0.0)
    count_u = jnp.minimum(count, west(count))
    count_v = jnp.minimum(count, south(count))
    depth_u = count_u + count_u * (count_u - 1.0) * (0.5 / levels)
    depth_v = count_v + count_v * (count_v - 1.0) * (0.5 / levels)
    cu, cv = squeeze(count_u), squeeze(count_v)
    row16 = lax.broadcasted_iota(jnp.int32, (2 * ROWS, 2 * COLS), 0)
    row16 = (r * ROWS + jnp.where(row16 < 12, row16, row16 - 16)).astype(jnp.float32)
    fu = 0.5 + (row16 + 0.5) / total_rows
    fv = 0.5 + row16 / total_rows

    whole(2, col_in).wait_recv()
    col_u = jnp.where(inside, around(col_out[0], lambda d: col_in[d, 0]), 0.0)
    col_v = jnp.where(inside, around(col_out[1], lambda d: col_in[d, 1]), 0.0)
    elevation = around(elev_ref[...], lambda d: elev_in[d])
    load = jnp.where(
        inside, elevation + GRAVITY_DT * (east(col_u) - col_u + north(col_v) - col_v), 0.0
    )

    def beyond_one(p):
        flow_u = depth_u * (p - west(p))
        flow_v = depth_v * (p - south(p))
        return -GRAVITY_DT * (east(flow_u) - flow_u + north(flow_v) - flow_v)

    def operate(p):
        return p + beyond_one(p)

    sub16 = lax.broadcasted_iota(jnp.int32, (16, COLS), 0)
    lane16 = lax.broadcasted_iota(jnp.int32, (16, COLS), 1)
    lane1 = lax.broadcasted_iota(jnp.int32, (1, COLS), 1)

    def dots(pairs):
        sums = jnp.zeros((16, COLS), jnp.float32)
        for m, (a, b) in enumerate(pairs):
            part = jnp.sum(a[:ROWS, :COLS] * b[:ROWS, :COLS], axis=0, keepdims=True)
            sums = jnp.where(sub16 == m, part, sums)
        sums = jnp.sum(sums, axis=1, keepdims=True)
        return jnp.sum(jnp.where(lane16 == sub16, sums, 0.0), axis=0, keepdims=True)

    def tx_copy(i, o):
        return pltpu.make_async_remote_copy(
            src_ref=mine.at[2 * i], dst_ref=tx_in.at[i, o - 1],
            send_sem=send_sem.at[7 + i], recv_sem=recv_sem.at[7 + i],
            device_id=(r, lax.rem(c + o, n_tx)), device_id_type=MESH,
        )

    def ty_copy(i, o):
        return pltpu.make_async_remote_copy(
            src_ref=mine.at[2 * i + 1], dst_ref=ty_in.at[i, o - 1],
            send_sem=send_sem.at[9 + i], recv_sem=recv_sem.at[9 + i],
            device_id=(lax.rem(r + o, n_ty), c), device_id_type=MESH,
        )

    def total(i, row, cover_tx, cover_ty):
        mine[2 * i] = row
        for o in tx_order:
            tx_copy(i, o).start()
        cover_tx()
        whole(7 + i, tx_in.at[i]).wait_recv()
        row = row + jnp.sum(tx_in[i], axis=0)
        mine[2 * i + 1] = row
        for o in ty_order:
            ty_copy(i, o).start()
        cover_ty()
        whole(9 + i, ty_in.at[i]).wait_recv()
        return row + jnp.sum(ty_in[i], axis=0)

    def pick(row, m):
        return jnp.sum(jnp.where(lane1 == m, row, 0.0), axis=1, keepdims=True)

    inner = lax.rem(lane, 4) < 2
    low8 = sub < 4
    beside = jnp.where(inner, c, n_tx - 1 - c) > 0
    beyond = jnp.where(low8, n_ty - 1 - r, r) > 0

    def receive():
        for number, ref in ((3, row_in), (4, row2_in), (5, colp_in), (6, corner_in)):
            whole(number, ref).wait_recv()
        for f in range(6):
            side = jnp.where(inner, colp_in[0, f], colp_in[1, f])
            sides[f] = jnp.where(beside, side, 0.0)
        for f in range(4):
            upper = jnp.where(inner, corner_in[NW - NE, f], corner_in[NE - NE, f])
            lower = jnp.where(inner, corner_in[SW - NE, f], corner_in[SE - NE, f])
            corners[f] = jnp.where(beside & beyond, jnp.where(low8, upper, lower), 0.0)

    def prepare(k, carry):
        shift = lax.rem(126 - 4 * k + COLS, COLS)
        nb, sb = row_in[0, k], row_in[1, k]
        nb2, sb2 = row2_in[0, k], row2_in[1, k]

        def wide(f, ref, ends):
            side = pltpu.roll(sides[f], shift, 1)
            corner = pltpu.roll(corners[f], shift, 1) if f < 4 else side
            return tile(ref[k], side, jnp.where(beyond, ends, 0.0), corner)

        def both(f, ref):
            i = f - 2
            ends = jnp.where(
                low8,
                jnp.broadcast_to(nb2[i : i + 1], (ROWS, COLS)),
                jnp.broadcast_to(sb2[i : i + 1], (ROWS, COLS)),
            )
            return wide(f, ref, ends)

        u = wide(0, u_ref, jnp.where(low8, nb, sb))
        v = wide(1, v_ref, jnp.where(low8, turn(nb, -2, 0), turn(sb, 2, 0)))
        t = wide(4, t_ref, jnp.where(low8, turn(nb, 4, 0), turn(sb, 4, 0)))
        ts = wide(5, ts_ref, jnp.where(low8, turn(nb, 2, 0), turn(sb, -2, 0)))
        us = both(2, us_ref)
        vs = both(3, vs_ref)
        level = k.astype(jnp.float32)
        mask_u = jnp.where(cu > level, ADVECT, 0.0)
        mask_v = jnp.where(cv > level, ADVECT, 0.0)

        flux_x = mask_u * (ts - west(ts))
        flux_y = mask_v * (ts - south(ts))
        x, y = u * flux_x, v * flux_y
        xe, yn = east(x), north(y)
        gt = ts + (
            7.0 * (x + xe + y + yn) - (west(x) + east(xe) + south(y) + north(yn))
        ) * (1.0 / 12.0)
        gt_ref[k] = gt[:ROWS, :COLS]
        tw, tso = west(t), south(t)
        face_x = (7.0 * (t + tw) - (east(t) + west(tw))) * (1.0 / 12.0)
        face_y = (7.0 * (t + tso) - (north(t) + south(tso))) * (1.0 / 12.0)

        ue, vn = east(u), north(v)
        pair_v, pair_u = v + vn, u + ue
        v_bar = 0.25 * (pair_v + west(pair_v))
        u_bar = 0.25 * (pair_u + south(pair_u))
        ahead_x = 0.5 * mask_u * u
        ahead_y = 0.5 * mask_u * v_bar
        turning = 0.25 * mask_u * (fu - 0.5 * (north(u) - south(u)))
        own_mu, own_mv = mask_u[:ROWS, :COLS], mask_v[:ROWS, :COLS]
        ku = -0.5 * own_mu * (ue - west(u))[:ROWS, :COLS]
        kv = -0.5 * own_mv * (vn - south(v))[:ROWS, :COLS]
        u_cross = [ku, seen(ahead_x, CROSS[1]), -seen(ahead_x, CROSS[2]), seen(ahead_y, CROSS[3]), -seen(ahead_y, CROSS[4])]
        v_corners = [seen(turning, p) for p in V_CORNERS]
        ahead_y = 0.5 * mask_v * v
        ahead_x = 0.5 * mask_v * u_bar
        turning = -0.25 * mask_v * (fv + 0.5 * (east(v) - west(v)))
        v_cross = [kv, seen(ahead_x, CROSS[1]), -seen(ahead_x, CROSS[2]), seen(ahead_y, CROSS[3]), -seen(ahead_y, CROSS[4])]
        u_corners = [seen(turning, p) for p in U_CORNERS]
        us_at, vs_at = [seen(us, p) for p in CROSS], [seen(vs, p) for p in CROSS]
        gu = gather(u_cross + u_corners, us_at + [seen(vs, p) for p in U_CORNERS])
        gv = gather(v_cross + v_corners, vs_at + [seen(us, p) for p in V_CORNERS])
        gu_ref[k] = gu + us_at[0] + (flux_x * face_x)[:ROWS, :COLS]
        gv_ref[k] = gv + vs_at[0] + (flux_y * face_y)[:ROWS, :COLS]
        u_cross[0] = ku + jnp.where(own_mu > 0.0, 1.0, 0.0)
        v_cross[0] = kv + jnp.where(own_mv > 0.0, 1.0, 0.0)
        for m, weight in enumerate(u_cross + u_corners):
            u_weights[k, m] = weight
        for m, weight in enumerate(v_cross + v_corners):
            v_weights[k, m] = weight
        return carry

    third_of = levels // 3

    def cover_first():
        receive()
        lax.fori_loop(0, third_of, prepare, 0)

    p0 = load
    p1 = beyond_one(p0)
    p2 = beyond_one(p1)
    row = total(
        0, dots([(p0, p0), (p0, p1), (p1, p1), (p1, p2)]), lambda: None, cover_first
    )
    g00, g01, g11, g12 = [pick(row, m) for m in range(4)]
    alpha1 = g00 / (g00 + g01)
    rest1 = g01 / (g00 + g01)
    norm1 = rest1 * rest1 * g00 - 2.0 * rest1 * alpha1 * g01 + alpha1 * alpha1 * g11
    beta1 = norm1 / g00
    r_b_r = rest1 * rest1 * g01 - 2.0 * rest1 * alpha1 * g11 + alpha1 * alpha1 * g12
    alpha2 = norm1 / (norm1 + r_b_r - beta1 * norm1 / alpha1)
    r1 = rest1 * p0 - alpha1 * p1
    d1 = r1 + beta1 * p0
    x2 = alpha1 * p0 + alpha2 * d1
    w0 = r1 - alpha2 * (d1 + (rest1 + beta1) * p1 - alpha1 * p2)

    w1 = d1
    w2, w3 = operate(w0), operate(w1)
    w4, w5 = operate(w2), operate(w3)
    row = total(
        1,
        dots(
            [(w0, w0), (w0, w2), (w0, w3), (w1, w3), (w2, w2), (w2, w3), (w3, w3), (w2, w4), (w2, w5), (w3, w5)]
        ),
        lambda: lax.fori_loop(third_of, 2 * third_of, prepare, 0),
        lambda: lax.fori_loop(2 * third_of, levels, prepare, 0),
    )
    h00, h02, h03, h13, h22, h23, h33, h24, h25, h35 = [pick(row, m) for m in range(10)]
    beta2 = h00 / norm1
    twice, square = 2.0 * beta2, beta2 * beta2
    d_a_d = h02 + twice * h03 + square * h13
    ad_ad = h22 + twice * h23 + square * h33
    d_aaa_d = h24 + twice * h25 + square * h35
    r_a_d = h02 + beta2 * h03
    ar_ad = h22 + beta2 * h23
    alpha3 = h00 / d_a_d
    norm3 = h00 - 2.0 * alpha3 * r_a_d + alpha3 * alpha3 * ad_ad
    beta3 = norm3 / h00
    alpha4 = norm3 / (
        h02 + 2.0 * beta3 * r_a_d - 2.0 * alpha3 * ar_ad
        + beta3 * beta3 * d_a_d - 2.0 * alpha3 * beta3 * ad_ad + alpha3 * alpha3 * d_aaa_d
    )
    d2 = w0 + beta2 * w1
    d3 = w0 + beta3 * d2 - alpha3 * (w2 + beta2 * w3)
    answer = x2 + alpha3 * d2 + alpha4 * d3
    eta_ref[...] = answer[:ROWS, :COLS]
    slope_x, slope_y = answer - west(answer), answer - south(answer)
    for m, (slope, place) in enumerate(
        [(slope_x, p) for p in CROSS] + [(slope_y, p) for p in U_CORNERS]
        + [(slope_y, p) for p in CROSS] + [(slope_x, p) for p in V_CORNERS]
    ):
        slope_ref[m] = seen(slope, place)

    for number, ref in (
        (0, count_in.at[0:2]), (11, count_in.at[2:8]), (1, elev_in), (2, col_in), (3, row_in), (4, row2_in), (5, colp_in), (6, corner_in),
        (7, tx_in.at[0]), (8, tx_in.at[1]), (9, ty_in.at[0]), (10, ty_in.at[1]),
    ):
        whole(number, ref).wait_send()


def finish(
    levels, pieces,
    gu_ref, gv_ref, gt_ref, eta_ref, slope_ref, u_weights, v_weights,
    gu_hbm, gv_hbm, gt_hbm, eta_hbm,
    gu_out, gv_out, sems,
):
    copies = [
        pltpu.make_async_copy(gt_ref, gt_hbm, sems.at[0]),
        pltpu.make_async_copy(eta_ref, eta_hbm, sems.at[1]),
    ]
    for copy in copies:
        copy.start()
    slopes = [slope_ref[m] for m in range(18)]

    def level(k, carry):
        thick = 1.0 + k.astype(jnp.float32) * (1.0 / levels)
        gu_out[k] = gu_ref[k] + thick * gather([u_weights[k, m] for m in range(9)], slopes[:9])
        gv_out[k] = gv_ref[k] + thick * gather([v_weights[k, m] for m in range(9)], slopes[9:])
        return carry

    size = levels // pieces
    for i in range(pieces):
        lax.fori_loop(i * size, (i + 1) * size, level, 0)
        part = pl.ds(i * size, size)
        for g, (src, dst) in enumerate(((gu_out, gu_hbm), (gv_out, gv_hbm))):
            copy = pltpu.make_async_copy(src.at[part], dst.at[part], sems.at[2 + 2 * i + g])
            copy.start()
            copies.append(copy)
    for copy in copies:
        copy.wait()


def on_device(n_ty, n_tx, u, v, t, count, us, vs, ts, elevation):
    levels = u.shape[0]
    f32 = jnp.float32
    block = jax.ShapeDtypeStruct(u.shape, f32)
    face = jax.ShapeDtypeStruct(elevation.shape, f32)
    weights = jax.ShapeDtypeStruct((levels, 9, ROWS, COLS), f32)
    slopes = jax.ShapeDtypeStruct((18, ROWS, COLS), f32)
    own = pltpu.VMEM((levels, ROWS, COLS), f32)
    two = pltpu.VMEM((levels, 2, COLS), f32)
    tiles = lambda *n, dtype=f32: pltpu.VMEM((*n, ROWS, COLS), dtype)
    vmem, hbm = pl.BlockSpec(memory_space=pltpu.VMEM), pl.BlockSpec(memory_space=pltpu.HBM)
    parts = pl.pallas_call(
        functools.partial(kernel, levels, n_ty, n_tx),
        out_shape=(block, block, block, face, slopes, weights, weights),
        in_specs=[hbm] * 8,
        out_specs=[vmem] * 7,
        scratch_shapes=[
            own, own, own, own, own, own, tiles(dtype=jnp.int32), tiles(),
            tiles(8, dtype=jnp.int32), tiles(8), tiles(2), tiles(8, 2),
            tiles(6), tiles(2, 6), tiles(4, 4), own, own, two, two,
            tiles(2, levels), pltpu.VMEM((2, levels, 2, COLS), f32),
            tiles(6), tiles(4),
            pltpu.VMEM((4, 1, COLS), f32),
            pltpu.VMEM((2, n_tx - 1, 1, COLS), f32),
            pltpu.VMEM((2, n_ty - 1, 1, COLS), f32),
            pltpu.SemaphoreType.DMA((8,)),
            pltpu.SemaphoreType.DMA((12,)),
            pltpu.SemaphoreType.DMA((12,)),
        ],
        compiler_params=pltpu.CompilerParams(
            collective_id=0, has_side_effects=True, vmem_limit_bytes=32 * 1024 * 1024
        ),
    )(*[pltpu.with_memory_space_constraint(x, pltpu.HBM) for x in (u, v, t, count, us, vs, ts, elevation)])
    pieces = 3
    return pl.pallas_call(
        functools.partial(finish, levels, pieces),
        out_shape=(block, block, block, face),
        in_specs=[vmem] * 7,
        out_specs=[hbm] * 4,
        scratch_shapes=[own, own, pltpu.SemaphoreType.DMA((2 + 2 * pieces,))],
        compiler_params=pltpu.CompilerParams(vmem_limit_bytes=16 * 1024 * 1024),
    )(*parts)


def solution(mesh):
    field, surface = P(None, "ty", "tx"), P("ty", "tx")
    return jax.shard_map(
        functools.partial(on_device, mesh.shape["ty"], mesh.shape["tx"]),
        mesh=mesh,
        in_specs=(field, field, field, surface, field, field, field, surface),
        out_specs=(field, field, field, surface),
        check_vma=False,
    )
```
